128 devices in a mesh: gx: 8 (over x, core), gy: 4 (over z), band: 4 (over y).
Axes of the slice: x: 4, y: 4, z: 4, core: 2. Of those that a mesh axis runs over, the one named last changes fastest.
Arguments:
- block: float32 [32, 96, 18432], P('band', 'gx', 'gy'), may hold values from -9 to 9
- prior: float32 [256, 96, 18432], P('band', 'gx', 'gy'), may hold values from -9 to 9
- potential: float32 [96, 18432], P('gx', 'gy'), may hold values from -1.5 to 1
Outputs:
- orbitals: float32 [32, 96, 18432], P('band', 'gx', 'gy')
The draws below stay inside these ranges and needn't reach their ends.
All inputs are finite; a program needn't handle non-finite values.
Results may differ from the reference program's by a relative error of at most 0.000098.
Values sent between devices are 32-bit elements; how exact they have to be, the bound alone decides.
A program may use at most 128 MiB of HBM per device.

```python
import jax
import jax.numpy as jnp
from jax import lax

NBLOCK = 32
NPRIOR = 256
NZ = 192
NX = 96
NY = 96
NCELLS = 1769472


def prior_base(key):
    shape = (NPRIOR, NX, NY * NZ)
    return jnp.clip(jax.random.normal(jax.random.fold_in(key, 11), shape, jnp.float32), -6.0, 6.0)


def draw_prior(key, part):
    return prior_base(key)


def draw_block(key, part):
    chosen = prior_base(key)[::NPRIOR // NBLOCK][:NBLOCK]
    fresh = jnp.clip(jax.random.normal(jax.random.fold_in(key, 13), (NBLOCK, NX, NY * NZ), jnp.float32), -6.0, 6.0)
    return 0.6 * fresh + 0.8 * chosen


def steps_of(stream_key, shape, split, smallest, largest):
    def one(axis_at, shards_of):
        heights = jax.random.uniform(jax.random.fold_in(jax.random.fold_in(stream_key, 6), axis_at), (shards_of,), jnp.float32, smallest / len(split), largest / len(split))
        return jnp.repeat(jnp.exp(heights), shape[axis_at] // shards_of).reshape((-1,) + (1,) * (len(shape) - axis_at - 1))

    gain = one(*split[0])
    for cut in split[1:]:
        gain = gain * one(*cut)
    return gain


def setup_inputs(seed: int = 0) -> dict:
    seeds = jax.random.split(jax.random.key(seed), 4)
    block = draw_block(jax.random.fold_in(seeds[3], 71), 0)
    prior = draw_prior(jax.random.fold_in(seeds[3], 71), 0)
    potential = jnp.clip(-1.5 + 2.5 * jax.random.uniform(seeds[2], (NX, NY * NZ), jnp.float32) ** steps_of(seeds[2], (NX, NY * NZ), ((0, 8), (1, 4)), -0.2, 0.2), -1.5, 1.0)
    return {"block": block, "prior": prior, "potential": potential}


coeffs = (-205.0 / 72.0, 8.0 / 5.0, -1.0 / 5.0, 8.0 / 315.0, -1.0 / 560.0)

def laplace(padded):
    center = padded[:, 4:-4, 4:-4, 4:-4]
    total = 3.0 * coeffs[0] * center
    for shift in range(1, 5):
        total = total + coeffs[shift] * (padded[:, 4 + shift:padded.shape[1] - 4 + shift, 4:-4, 4:-4] + padded[:, 4 - shift:padded.shape[1] - 4 - shift, 4:-4, 4:-4])
        total = total + coeffs[shift] * (padded[:, 4:-4, 4 + shift:padded.shape[2] - 4 + shift, 4:-4] + padded[:, 4:-4, 4 - shift:padded.shape[2] - 4 - shift, 4:-4])
        total = total + coeffs[shift] * (padded[:, 4:-4, 4:-4, 4 + shift:padded.shape[3] - 4 + shift] + padded[:, 4:-4, 4:-4, 4 - shift:padded.shape[3] - 4 - shift])
    return total

def reference(block, prior, potential):
    grid_block = block.reshape(NBLOCK, NX, NY, NZ)
    grid_pot = potential.reshape(NX, NY, NZ)
    padded = jnp.pad(grid_block, ((0, 0), (4, 4), (4, 4), (4, 4)))
    phi = -2.0 * laplace(padded) + grid_pot[None] * grid_block
    phi_flat = phi.reshape(NBLOCK, -1)
    prior_flat = prior.reshape(NPRIOR, -1)
    correlation = jnp.dot(prior_flat.astype(jnp.float32), phi_flat.T.astype(jnp.float32), precision=lax.Precision.HIGHEST, preferred_element_type=jnp.float32) / NCELLS
    projected = phi_flat - jnp.dot(correlation.T.astype(jnp.float32), prior_flat.astype(jnp.float32), precision=lax.Precision.HIGHEST, preferred_element_type=jnp.float32)
    gram = jnp.dot(projected.astype(jnp.float32), projected.T.astype(jnp.float32), precision=lax.Precision.HIGHEST, preferred_element_type=jnp.float32) / NCELLS
    lower = jnp.linalg.cholesky(gram)
    inverse = lax.linalg.triangular_solve(lower, jnp.eye(NBLOCK, dtype=lower.dtype), left_side=True, lower=True)
    orbitals = jnp.dot(inverse.astype(jnp.float32), projected.astype(jnp.float32), precision=lax.Precision.HIGHEST, preferred_element_type=jnp.float32)
    return orbitals.reshape(block.shape)
```

```python
import functools

import jax
import jax.numpy as jnp
from jax import lax
from jax.experimental import pallas as pl
from jax.experimental.pallas import tpu as pltpu
from jax.sharding import PartitionSpec as P

NZ = 192
WIDTH = 4 * NZ
CHUNK = 2 * NZ
WIDE = 2 * CHUNK
F32 = jnp.float32
BF16 = jnp.bfloat16
MESH = pl.DeviceIdType.MESH

coeffs = (-205.0 / 72.0, 8.0 / 5.0, -1.0 / 5.0, 8.0 / 315.0, -1.0 / 560.0)


def halves(value):
    high = value.astype(BF16)
    low = (value - high.astype(F32)).astype(BF16)
    return jnp.concatenate([high, low], axis=0)


def dot(left, right):
    return jnp.dot(left, right, preferred_element_type=F32)


def dot_nt(left, right):
    return lax.dot_general(left, right, (((1,), (1,)), ((), ())), preferred_element_type=F32)


def remote(src, dst, send, recv, axis, peer):
    return pltpu.make_async_remote_copy(
        src_ref=src, dst_ref=dst, send_sem=send, recv_sem=recv, device_id={axis: peer}, device_id_type=MESH
    )


def all_reduce(value, stages, slots, send, recv):
    for at, axis, me, n in stages:
        slots[at, me] = value
        copies = []
        for k in range(1, n):
            copy = remote(
                slots.at[at, me], slots.at[at, me], send.at[at, k - 1], recv.at[at, k - 1], axis, lax.rem(me + k, n)
            )
            copy.start()
            copies.append(copy)
        for copy in copies:
            copy.wait()
        value = slots[at, 0]
        for k in range(1, n):
            value = value + slots[at, k]
    return value


def inverse_factor(gram):
    count = gram.shape[0]
    row = lax.broadcasted_iota(jnp.int32, gram.shape, 0)
    lane = lax.broadcasted_iota(jnp.int32, gram.shape, 1)
    table = jnp.where(lane < count, gram, jnp.where(lane - count == row, 1.0, 0.0))
    for k in range(count - 1):
        pivot = table[k : k + 1, :]
        factor = table[:, k : k + 1] / table[k : k + 1, k : k + 1]
        table = table - jnp.where(row > k, factor, 0.0) * pivot
    diagonal = jnp.sum(jnp.where(lane == row, table, 0.0), axis=1, keepdims=True)
    inverse = jnp.where((lane >= count) & (lane < 2 * count), table * (1.0 / jnp.sqrt(diagonal)), 0.0)
    return inverse + pltpu.roll(inverse, gram.shape[1] - count, axis=1)


def kernel(
    sizes, ncells, block, prior, potential, out,
    grid, phi, staged, stacked, product, opposite, sides, opposite_in, sides_in, projected, pieces, result, slots,
    local_sem, stage_sem, halo_send, halo_recv, ring_send, ring_recv, relay_send, relay_recv,
    opp_send, opp_recv, side_send, side_recv, sum_send, sum_recv, back_send, back_recv,
):
    nx, ny, nb = sizes
    gx, gy, band = lax.axis_index("gx"), lax.axis_index("gy"), lax.axis_index("band")
    planes, own, cells = block.shape
    quarter = planes // nb
    count = nb * own
    right, left, across = lax.rem(band + 1, nb), lax.rem(band + nb - 1, nb), lax.rem(band + 2, nb)

    fill = pltpu.make_async_copy(block, grid.at[pl.ds(4, planes), :, pl.ds(WIDTH, cells)], local_sem.at[0])
    fill.start()

    def stage(x, slot):
        return pltpu.make_async_copy(prior.at[x], staged.at[slot], stage_sem.at[slot])

    stage(0, 0).start()
    stage(1, 1).start()

    barrier = pltpu.get_barrier_semaphore()
    for axis, me, n in (("gx", gx, nx), ("gy", gy, ny), ("band", band, nb)):
        for k in range(1, n):
            pl.semaphore_signal(barrier, inc=1, device_id={axis: lax.rem(me + k, n)}, device_id_type=MESH)
    pl.semaphore_wait(barrier, nx + ny + nb - 3)

    middle = pl.ds(WIDTH, cells)
    inner = pl.ds(4, planes)
    halos = (
        (0, "gx", gx, nx, 1, block.at[pl.ds(planes - 4, 4)], grid.at[pl.ds(0, 4), :, middle]),
        (1, "gx", gx, nx, -1, block.at[pl.ds(0, 4)], grid.at[pl.ds(planes + 4, 4), :, middle]),
        (2, "gy", gy, ny, 1, block.at[:, :, pl.ds(cells - WIDTH, WIDTH)], grid.at[inner, :, pl.ds(0, WIDTH)]),
        (3, "gy", gy, ny, -1, block.at[:, :, pl.ds(0, WIDTH)], grid.at[inner, :, pl.ds(WIDTH + cells, WIDTH)]),
    )

    def halo(at, axis, me, n, step, src, dst):
        copy = remote(src, dst, halo_send.at[at], halo_recv.at[at], axis, lax.rem(me + step + n, n))
        sends, receives = (me < n - 1, me > 0) if step == 1 else (me > 0, me < n - 1)
        return copy, sends, receives, dst

    for entry in halos:
        copy, sends, receives, dst = halo(*entry)
        pl.when(sends)(copy.start)

    for entry in halos:
        copy, sends, receives, dst = halo(*entry)

        @pl.when(jnp.logical_not(receives))
        def _(dst=dst):
            dst[...] = jnp.zeros(dst.shape, F32)

    fill.wait()
    for entry in halos:
        copy, sends, receives, dst = halo(*entry)
        pl.when(receives)(copy.wait_recv)
        pl.when(sends)(copy.wait_send)

    depth = lax.rem(lax.broadcasted_iota(jnp.int32, (own, CHUNK), 1), NZ)
    ups = [jnp.where(depth < NZ - m, coeffs[m], 0.0).astype(F32) for m in range(1, 5)]
    downs = [jnp.where(depth >= m, coeffs[m], 0.0).astype(F32) for m in range(1, 5)]

    def to_right(x):
        return remote(phi.at[x, band], phi.at[x, band], ring_send.at[0, x], ring_recv.at[0, x], "band", right)

    def to_left(x):
        return remote(phi.at[x, band], phi.at[x, band], ring_send.at[1, x], ring_recv.at[1, x], "band", left)

    def hamiltonian(x, carry):
        for start in range(0, cells, CHUNK):
            s = WIDTH + start
            center = grid[x + 4, :, pl.ds(s, CHUNK)]
            total = 3.0 * coeffs[0] * center
            for m in range(1, 5):
                total = total + coeffs[m] * (
                    grid[x + 4 + m, :, pl.ds(s, CHUNK)] + grid[x + 4 - m, :, pl.ds(s, CHUNK)]
                )
            for m in (2, 4):
                total = total + coeffs[m] * (
                    grid[x + 4, :, pl.ds(s + m * NZ, CHUNK)] + grid[x + 4, :, pl.ds(s - m * NZ, CHUNK)]
                )
            odd = None
            for m in (1, 3):
                term = coeffs[m] * (
                    grid[x + 4, :, pl.ds(s + m * NZ - 64, CHUNK + 128)]
                    + grid[x + 4, :, pl.ds(s - m * NZ - 64, CHUNK + 128)]
                )
                odd = term if odd is None else odd + term
            total = total + pltpu.roll(odd, CHUNK + 64, axis=1)[:, :CHUNK]
            for m in range(1, 5):
                total = total + ups[m - 1] * pltpu.roll(center, CHUNK - m, axis=1)
                total = total + downs[m - 1] * pltpu.roll(center, m, axis=1)
            weight = potential[pl.ds(x, 1), pl.ds(start, CHUNK)]
            phi[x, band, :, pl.ds(start, CHUNK)] = weight * center - 2.0 * total
        to_right(x).start()
        to_left(x).start()
        return carry

    lax.fori_loop(0, planes, hamiltonian, 0)

    def relay_right(x):
        return remote(phi.at[x, left], phi.at[x, left], relay_send.at[x], relay_recv.at[x], "band", right)

    def relay_left(x):
        return remote(phi.at[x, right], phi.at[x, right], relay_send.at[x], relay_recv.at[x], "band", left)

    product[...] = jnp.zeros_like(product)
    pairs = planes // 2

    def gather(i, carry):
        @pl.when(i < pairs)
        def _():
            for slot, relay in ((0, relay_right), (1, relay_left)):
                x = 2 * i + slot
                stage(x, slot).wait()
                stacked[x] = halves(staged[slot])

                @pl.when(i < pairs - 1)
                def _(x=x, slot=slot):
                    stage(x + 2, slot).start()

                to_right(x).wait_recv()
                to_left(x).wait_recv()
                relay(x).start()

        @pl.when(i > 0)
        def _():
            for slot, relay in ((0, relay_right), (1, relay_left)):
                x = 2 * i - 2 + slot
                relay(x).wait_recv()
                relay(x).wait_send()
                to_right(x).wait_send()
                to_left(x).wait_send()
                product[...] += dot_nt(halves(phi[x].reshape(count, cells)), stacked[x])

        return carry

    lax.fori_loop(0, pairs + 1, gather, 0)

    folded = product[pl.ds(0, count), :] + product[pl.ds(count, count), :]
    folded = folded + pltpu.roll(folded, 64, axis=1)
    correlation = all_reduce(folded, ((0, "gx", gx, nx), (1, "gy", gy, ny)), slots, sum_send, sum_recv)
    weights = halves(correlation * (1.0 / ncells))

    def removed(x, store):
        for start in range(0, cells, WIDE):
            both = dot(weights, stacked[x, :, pl.ds(start, WIDE)])
            store(start, both[:count] + both[count:])

    half = count // 2

    def across_copies(p):
        return (
            remote(opposite.at[p, pl.ds(0, half)], opposite_in.at[0, p], opp_send.at[0, p], opp_recv.at[0, p], "band", right),
            remote(opposite.at[p, pl.ds(half, half)], opposite_in.at[1, p], opp_send.at[1, p], opp_recv.at[1, p], "band", left),
        )

    def side_copy(side, p):
        return remote(sides.at[side, p], sides_in.at[side, p], side_send.at[side, p], side_recv.at[side, p], "band", (right, left)[side])

    def send_across(p, carry):
        def store(start, value):
            opposite[p, :, pl.ds(start, WIDE)] = value

        removed(across * quarter + p, store)
        for copy in across_copies(p):
            copy.start()
        return carry

    lax.fori_loop(0, quarter, send_across, 0)

    def send_sides(p, carry):
        for side in range(2):

            def store(start, value, side=side):
                sides[side, p, :, pl.ds(start, WIDE)] = value

            removed((right, left)[side] * quarter + p, store)
        for side in range(2):
            copy = across_copies(p)[side]
            copy.wait_recv()
            copy.wait_send()
            sides[side, p, pl.ds(side * half, half)] += opposite_in[side, p]
            side_copy(side, p).start()
        return carry

    lax.fori_loop(0, quarter, send_sides, 0)

    def own_part(p, carry):
        x = band * quarter + p

        def store(start, value):
            projected[p, :, pl.ds(start, WIDE)] = phi[x, :, :, pl.ds(start, WIDE)].reshape(count, WIDE) - value

        removed(x, store)
        return carry

    lax.fori_loop(0, quarter, own_part, 0)

    product[...] = jnp.zeros_like(product)

    def inner_products(p, carry):
        for side in range(2):
            side_copy(side, p).wait_recv()
            side_copy(side, p).wait_send()
        for start in range(0, cells, WIDE):
            at = pl.ds(start, WIDE)
            pieces[p, :, at] = halves(projected[p, :, at] - (sides_in[0, p, :, at] + sides_in[1, p, :, at]))
        both = pieces[p]
        product[...] += dot_nt(both, jnp.concatenate([both, both], axis=0))
        return carry

    lax.fori_loop(0, quarter, inner_products, 0)

    folded = product[pl.ds(0, count), :] + product[pl.ds(count, count), :]
    folded = folded + pltpu.roll(folded, count, axis=1)
    gram = all_reduce(
        folded, ((2, "gx", gx, nx), (3, "gy", gy, ny), (4, "band", band, nb)), slots, sum_send, sum_recv
    )
    inverse = halves(inverse_factor(gram * (1.0 / ncells)))[:, : 2 * count]

    def back(p, k):
        return remote(
            result.at[p, lax.rem(band + k, nb)], out.at[band * quarter + p],
            back_send.at[p, k - 1], back_recv.at[p, k - 1], "band", lax.rem(band + k, nb),
        )

    def keep(p):
        return pltpu.make_async_copy(result.at[p, band], out.at[band * quarter + p], local_sem.at[p])

    def finish(p, carry):
        for start in range(0, cells, WIDE):
            at = pl.ds(start, WIDE)
            both = dot(inverse, pieces[p, :, at])
            result[p, :, :, at] = (both[:count] + both[count:]).reshape(nb, own, WIDE)
        for k in (2, 1, 3):
            back(p, k).start()
        keep(p).start()
        return carry

    lax.fori_loop(0, quarter, finish, 0)

    def drain(p, carry):
        for k in range(1, nb):
            back(p, k).wait()
        keep(p).wait()
        return carry

    lax.fori_loop(0, quarter, drain, 0)


def shards(sizes, block, prior, potential):
    nx, ny, nb = sizes
    block_x, prior_x = block.transpose(1, 0, 2), prior.transpose(1, 0, 2)
    planes, own, cells = block_x.shape
    priors, count, quarter = prior_x.shape[1], own * nb, planes // nb
    ncells = planes * nx * cells * ny
    dma = pltpu.SemaphoreType.DMA
    most = max(sizes)
    out = pl.pallas_call(
        functools.partial(kernel, sizes, ncells),
        out_shape=jax.ShapeDtypeStruct(block_x.shape, F32),
        in_specs=[
            pl.BlockSpec(memory_space=pl.ANY),
            pl.BlockSpec(memory_space=pl.ANY),
            pl.BlockSpec(memory_space=pltpu.VMEM),
        ],
        out_specs=pl.BlockSpec(memory_space=pl.ANY),
        scratch_shapes=[
            pltpu.VMEM((planes + 8, own, cells + 2 * WIDTH), F32),
            pltpu.VMEM((planes, nb, own, cells), F32),
            pltpu.VMEM((2, priors, cells), F32),
            pltpu.VMEM((planes, 2 * priors, cells), BF16),
            pltpu.VMEM((2 * count, 128), F32),
            pltpu.VMEM((quarter, count, cells), F32),
            pltpu.VMEM((2, quarter, count, cells), F32),
            pltpu.VMEM((2, quarter, count // 2, cells), F32),
            pltpu.VMEM((2, quarter, count, cells), F32),
            pltpu.VMEM((quarter, count, cells), F32),
            pltpu.VMEM((quarter, 2 * count, cells), BF16),
            pltpu.VMEM((quarter, nb, own, cells), F32),
            pltpu.VMEM((5, most, count, 128), F32),
            dma((quarter,)),
            dma((2,)),
            dma((4,)),
            dma((4,)),
            dma((2, planes)),
            dma((2, planes)),
            dma((planes,)),
            dma((planes,)),
            dma((2, quarter)),
            dma((2, quarter)),
            dma((2, quarter)),
            dma((2, quarter)),
            dma((5, most)),
            dma((5, most)),
            dma((quarter, nb)),
            dma((quarter, nb)),
        ],
        compiler_params=pltpu.CompilerParams(
            collective_id=0, has_side_effects=True, vmem_limit_bytes=67000000
        ),
    )(block_x, prior_x, potential)
    return out.transpose(1, 0, 2)


def solution(mesh):
    sizes = tuple(mesh.shape[a] for a in ("gx", "gy", "band"))
    in_specs = (P("band", "gx", "gy"), P("band", "gx", "gy"), P("gx", "gy"))
    out_specs = P("band", "gx", "gy")
    return jax.shard_map(
        functools.partial(shards, sizes), mesh=mesh, in_specs=in_specs, out_specs=out_specs, check_vma=False
    )
```

```python
import functools

import jax
import jax.numpy as jnp
from jax import lax
from jax.experimental import pallas as pl
from jax.experimental.pallas import tpu as pltpu
from jax.sharding import PartitionSpec as P

NZ = 192
WIDTH = 4 * NZ
CHUNK = 2 * NZ
WIDE = 2 * CHUNK
F32 = jnp.float32
BF16 = jnp.bfloat16
MESH = pl.DeviceIdType.MESH

coeffs = (-205.0 / 72.0, 8.0 / 5.0, -1.0 / 5.0, 8.0 / 315.0, -1.0 / 560.0)


def halves(value):
    high = value.astype(BF16)
    low = (value - high.astype(F32)).astype(BF16)
    return jnp.concatenate([high, low], axis=0)


def dot(left, right):
    return jnp.dot(left, right, preferred_element_type=F32)


def dot_nt(left, right):
    return lax.dot_general(left, right, (((1,), (1,)), ((), ())), preferred_element_type=F32)


def remote(src, dst, send, recv, axis, peer):
    return pltpu.make_async_remote_copy(
        src_ref=src, dst_ref=dst, send_sem=send, recv_sem=recv, device_id={axis: peer}, device_id_type=MESH
    )


def all_reduce(value, stages, slots, send, recv):
    rows = pl.ds(0, value.shape[0])
    for at, axis, me, n in stages:
        slots[at, me, rows] = value
        copies = []
        for k in range(1, n):
            copy = remote(
                slots.at[at, me, rows], slots.at[at, me, rows], send.at[at, k - 1], recv.at[at, k - 1], axis, lax.rem(me + k, n)
            )
            copy.start()
            copies.append(copy)
        for copy in copies:
            copy.wait()
        value = slots[at, 0, rows]
        for k in range(1, n):
            value = value + slots[at, k, rows]
    return value


def pack(value, parts):
    rows, lanes = value.shape[0] // parts, value.shape[1] // parts
    group = lax.broadcasted_iota(jnp.int32, (rows, value.shape[1]), 1) // lanes
    packed = value[:rows]
    for k in range(1, parts):
        packed = jnp.where(group == k, value[k * rows : (k + 1) * rows], packed)
    return packed


def unpack(packed, parts):
    width = packed.shape[1]
    moved = [packed] + [pltpu.roll(packed, width - k * (width // parts), axis=1) for k in range(1, parts)]
    return jnp.concatenate(moved, axis=0)


def inverse_factor(gram):
    count = gram.shape[0]
    row = lax.broadcasted_iota(jnp.int32, gram.shape, 0)
    lane = lax.broadcasted_iota(jnp.int32, gram.shape, 1)
    table = jnp.where(lane < count, gram, jnp.where(lane - count == row, 1.0, 0.0))
    for k in range(count - 1):
        pivot = table[k : k + 1, :]
        factor = table[:, k : k + 1] / table[k : k + 1, k : k + 1]
        table = table - jnp.where(row > k, factor, 0.0) * pivot
    diagonal = jnp.sum(jnp.where(lane == row, table, 0.0), axis=1, keepdims=True)
    inverse = jnp.where((lane >= count) & (lane < 2 * count), table * (1.0 / jnp.sqrt(diagonal)), 0.0)
    return inverse + pltpu.roll(inverse, gram.shape[1] - count, axis=1)


def kernel(
    sizes, ncells, block, prior, potential, out,
    grid, phi, staged, stacked, product, opposite, sides, opposite_in, sides_in, projected, pieces, result, passing, slots,
    local_sem, stage_sem, halo_send, halo_recv, ring_send, ring_recv, relay_send, relay_recv,
    opp_send, opp_recv, side_send, side_recv, sum_send, sum_recv, back_send, back_recv,
    hop_send, hop_recv, last_send, last_recv,
):
    nx, ny, nb = sizes
    gx, gy, band = lax.axis_index("gx"), lax.axis_index("gy"), lax.axis_index("band")
    planes, own, cells = block.shape
    quarter = planes // nb
    count = nb * own
    right, left, across = lax.rem(band + 1, nb), lax.rem(band + nb - 1, nb), lax.rem(band + 2, nb)

    fill = pltpu.make_async_copy(block, grid.at[pl.ds(4, planes), :, pl.ds(WIDTH, cells)], local_sem.at[0])
    fill.start()

    def stage(x, slot):
        return pltpu.make_async_copy(prior.at[x], staged.at[slot], stage_sem.at[slot])

    stage(4, 0).start()
    stage(5, 1).start()

    barrier = pltpu.get_barrier_semaphore()
    for axis, me, n in (("gx", gx, nx), ("gy", gy, ny), ("band", band, nb)):
        for k in range(1, n):
            pl.semaphore_signal(barrier, inc=1, device_id={axis: lax.rem(me + k, n)}, device_id_type=MESH)
    pl.semaphore_wait(barrier, nx + ny + nb - 3)

    middle = pl.ds(WIDTH, cells)
    low, high = pl.ds(0, WIDTH), pl.ds(cells - WIDTH, WIDTH)
    above = pl.ds(WIDTH + cells, WIDTH)

    def y_halos(at, first, size):
        here, there = pl.ds(first, size), pl.ds(4 + first, size)
        return (
            (at, "gy", gy, ny, 1, block.at[here, :, high], grid.at[there, :, low]),
            (at + 1, "gy", gy, ny, -1, block.at[here, :, low], grid.at[there, :, above]),
        )

    halos = (
        *y_halos(0, 4, planes - 8),
        (2, "gx", gx, nx, 1, block.at[pl.ds(planes - 4, 4)], grid.at[pl.ds(0, 4), :, middle]),
        (3, "gx", gx, nx, -1, block.at[pl.ds(0, 4)], grid.at[pl.ds(planes + 4, 4), :, middle]),
        *y_halos(4, planes - 4, 4),
        *y_halos(6, 0, 4),
    )

    def halo(at, axis, me, n, step, src, dst):
        copy = remote(src, dst, halo_send.at[at], halo_recv.at[at], axis, lax.rem(me + step + n, n))
        sends, receives = (me < n - 1, me > 0) if step == 1 else (me > 0, me < n - 1)
        return copy, sends, receives, dst

    for entry in halos:
        copy, sends, receives, dst = halo(*entry)
        pl.when(sends)(copy.start)

    for entry in halos:
        copy, sends, receives, dst = halo(*entry)

        @pl.when(jnp.logical_not(receives))
        def _(dst=dst):
            dst[...] = jnp.zeros(dst.shape, F32)

    fill.wait()

    def arrive(entries):
        for entry in entries:
            copy, sends, receives, dst = halo(*entry)
            pl.when(receives)(copy.wait_recv)
            pl.when(sends)(copy.wait_send)

    depth = lax.rem(lax.broadcasted_iota(jnp.int32, (own, CHUNK), 1), NZ)
    ups = [jnp.where(depth < NZ - m, coeffs[m], 0.0).astype(F32) for m in range(1, 5)]
    downs = [jnp.where(depth >= m, coeffs[m], 0.0).astype(F32) for m in range(1, 5)]

    def to_right(x):
        return remote(phi.at[x, band], phi.at[x, band], ring_send.at[0, x], ring_recv.at[0, x], "band", right)

    def to_left(x):
        return remote(phi.at[x, band], phi.at[x, band], ring_send.at[1, x], ring_recv.at[1, x], "band", left)

    def place(i):
        return lax.rem(i + 4, planes)

    def hamiltonian(i, carry):
        x = place(i)
        for start in range(0, cells, CHUNK):
            s = WIDTH + start
            center = grid[x + 4, :, pl.ds(s, CHUNK)]
            total = 3.0 * coeffs[0] * center
            for m in range(1, 5):
                total = total + coeffs[m] * (
                    grid[x + 4 + m, :, pl.ds(s, CHUNK)] + grid[x + 4 - m, :, pl.ds(s, CHUNK)]
                )
            for m in (2, 4):
                total = total + coeffs[m] * (
                    grid[x + 4, :, pl.ds(s + m * NZ, CHUNK)] + grid[x + 4, :, pl.ds(s - m * NZ, CHUNK)]
                )
            odd = None
            for m in (1, 3):
                term = coeffs[m] * (
                    grid[x + 4, :, pl.ds(s + m * NZ - 64, CHUNK + 128)]
                    + grid[x + 4, :, pl.ds(s - m * NZ - 64, CHUNK + 128)]
                )
                odd = term if odd is None else odd + term
            total = total + pltpu.roll(odd, CHUNK + 64, axis=1)[:, :CHUNK]
            for m in range(1, 5):
                total = total + ups[m - 1] * pltpu.roll(center, CHUNK - m, axis=1)
                total = total + downs[m - 1] * pltpu.roll(center, m, axis=1)
            weight = potential[pl.ds(x, 1), pl.ds(start, CHUNK)]
            phi[x, band, :, pl.ds(start, CHUNK)] = weight * center - 2.0 * total
        to_right(x).start()
        to_left(x).start()
        return carry

    arrive(halos[:2])
    lax.fori_loop(0, planes - 8, hamiltonian, 0)
    arrive(halos[2:])
    lax.fori_loop(planes - 8, planes, hamiltonian, 0)

    def relay_right(x):
        return remote(phi.at[x, left], phi.at[x, left], relay_send.at[x], relay_recv.at[x], "band", right)

    def relay_left(x):
        return remote(phi.at[x, right], phi.at[x, right], relay_send.at[x], relay_recv.at[x], "band", left)

    product[...] = jnp.zeros_like(product)
    pairs = planes // 2

    def gather(i, carry):
        @pl.when(i < pairs)
        def _():
            for slot, relay in ((0, relay_right), (1, relay_left)):
                x = place(2 * i + slot)
                stage(x, slot).wait()
                stacked[x] = halves(staged[slot])

                @pl.when(i < pairs - 1)
                def _(x=x, slot=slot):
                    stage(lax.rem(x + 2, planes), slot).start()

                to_right(x).wait_recv()
                to_left(x).wait_recv()
                relay(x).start()

        @pl.when(i > 0)
        def _():
            for slot, relay in ((0, relay_right), (1, relay_left)):
                x = place(2 * i - 2 + slot)
                relay(x).wait_recv()
                relay(x).wait_send()
                to_right(x).wait_send()
                to_left(x).wait_send()
                product[...] += dot_nt(halves(phi[x].reshape(count, cells)), stacked[x])

        return carry

    lax.fori_loop(0, pairs + 1, gather, 0)

    folded = product[pl.ds(0, count), :] + product[pl.ds(count, count), :]
    folded = folded + pltpu.roll(folded, 64, axis=1)
    packed = all_reduce(pack(folded, 2), ((0, "gx", gx, nx), (1, "gy", gy, ny)), slots, sum_send, sum_recv)
    correlation = unpack(packed, 2) * (1.0 / ncells)
    lane = lax.broadcasted_iota(jnp.int32, correlation.shape, 1)
    correlation = jnp.where(lane < 64, correlation, pltpu.roll(correlation, 64, axis=1))
    weights = halves(correlation)

    def removed(x, store):
        for start in range(0, cells, WIDE):
            both = dot(weights, stacked[x, :, pl.ds(start, WIDE)])
            store(start, both[:count] + both[count:])

    half = count // 2

    def across_copies(p):
        return (
            remote(opposite.at[p, pl.ds(0, half)], opposite_in.at[0, p], opp_send.at[0, p], opp_recv.at[0, p], "band", right),
            remote(opposite.at[p, pl.ds(half, half)], opposite_in.at[1, p], opp_send.at[1, p], opp_recv.at[1, p], "band", left),
        )

    def side_copy(side, p):
        return remote(sides.at[side, p], sides_in.at[side, p], side_send.at[side, p], side_recv.at[side, p], "band", (right, left)[side])

    def send_across(p, carry):
        def store(start, value):
            opposite[p, :, pl.ds(start, WIDE)] = value

        removed(across * quarter + p, store)
        for copy in across_copies(p):
            copy.start()
        return carry

    lax.fori_loop(0, quarter, send_across, 0)

    def send_sides(p, carry):
        for side in range(2):

            def store(start, value, side=side):
                sides[side, p, :, pl.ds(start, WIDE)] = value

            removed((right, left)[side] * quarter + p, store)
        for side in range(2):
            copy = across_copies(p)[side]
            copy.wait_recv()
            copy.wait_send()
            sides[side, p, pl.ds(side * half, half)] += opposite_in[side, p]
            side_copy(side, p).start()
        return carry

    lax.fori_loop(0, quarter, send_sides, 0)

    def own_part(p, carry):
        x = band * quarter + p

        def store(start, value):
            projected[p, :, pl.ds(start, WIDE)] = phi[x, :, :, pl.ds(start, WIDE)].reshape(count, WIDE) - value

        removed(x, store)
        return carry

    lax.fori_loop(0, quarter, own_part, 0)

    product[...] = jnp.zeros_like(product)

    def inner_products(p, carry):
        for side in range(2):
            side_copy(side, p).wait_recv()
            side_copy(side, p).wait_send()
        for start in range(0, cells, WIDE):
            at = pl.ds(start, WIDE)
            pieces[p, :, at] = halves(projected[p, :, at] - (sides_in[0, p, :, at] + sides_in[1, p, :, at]))
        both = pieces[p]
        product[...] += dot_nt(both, jnp.concatenate([both, both], axis=0))
        return carry

    lax.fori_loop(0, quarter, inner_products, 0)

    folded = product[pl.ds(0, count), :] + product[pl.ds(count, count), :]
    folded = folded + pltpu.roll(folded, count, axis=1)
    packed = all_reduce(
        pack(folded, 4), ((2, "gx", gx, nx), (3, "gy", gy, ny), (4, "band", band, nb)), slots, sum_send, sum_recv
    )
    inverse = halves(inverse_factor(unpack(packed, 4) * (1.0 / ncells)))[:, : 2 * count]

    split = cells // 2

    def back(p, side):
        peer = (right, left)[side]
        return remote(
            result.at[p, peer], out.at[band * quarter + p], back_send.at[side, p], back_recv.at[side, p], "band", peer
        )

    def first_hop(p, side):
        part = pl.ds(side * split, split)
        return remote(
            result.at[p, across, :, part], passing.at[side, p],
            hop_send.at[side, p], hop_recv.at[side, p], "band", (right, left)[side],
        )

    def second_hop(p, side):
        part = pl.ds(side * split, split)
        return remote(
            passing.at[side, p], out.at[(left, right)[side] * quarter + p, :, part],
            last_send.at[side, p], last_recv.at[side, p], "band", (right, left)[side],
        )

    def keep(p):
        return pltpu.make_async_copy(result.at[p, band], out.at[band * quarter + p], local_sem.at[p])

    def finish(p, carry):
        for start in range(0, cells, WIDE):
            at = pl.ds(start, WIDE)
            both = dot(inverse, pieces[p, :, at])
            result[p, :, :, at] = (both[:count] + both[count:]).reshape(nb, own, WIDE)
        for side in range(2):
            first_hop(p, side).start()
        for side in range(2):
            back(p, side).start()
        keep(p).start()
        return carry

    lax.fori_loop(0, quarter, finish, 0)

    def forward(p, carry):
        for side in range(2):
            first_hop(p, side).wait()
            second_hop(p, side).start()
        return carry

    lax.fori_loop(0, quarter, forward, 0)

    def drain(p, carry):
        for side in range(2):
            back(p, side).wait()
            second_hop(p, side).wait()
        keep(p).wait()
        return carry

    lax.fori_loop(0, quarter, drain, 0)


def shards(sizes, block, prior, potential):
    nx, ny, nb = sizes
    block_x, prior_x = block.transpose(1, 0, 2), prior.transpose(1, 0, 2)
    planes, own, cells = block_x.shape
    priors, count, quarter = prior_x.shape[1], own * nb, planes // nb
    ncells = planes * nx * cells * ny
    dma = pltpu.SemaphoreType.DMA
    most = max(sizes)
    out = pl.pallas_call(
        functools.partial(kernel, sizes, ncells),
        out_shape=jax.ShapeDtypeStruct(block_x.shape, F32),
        in_specs=[
            pl.BlockSpec(memory_space=pl.ANY),
            pl.BlockSpec(memory_space=pl.ANY),
            pl.BlockSpec(memory_space=pltpu.VMEM),
        ],
        out_specs=pl.BlockSpec(memory_space=pl.ANY),
        scratch_shapes=[
            pltpu.VMEM((planes + 8, own, cells + 2 * WIDTH), F32),
            pltpu.VMEM((planes, nb, own, cells), F32),
            pltpu.VMEM((2, priors, cells), F32),
            pltpu.VMEM((planes, 2 * priors, cells), BF16),
            pltpu.VMEM((2 * count, 128), F32),
            pltpu.VMEM((quarter, count, cells), F32),
            pltpu.VMEM((2, quarter, count, cells), F32),
            pltpu.VMEM((2, quarter, count // 2, cells), F32),
            pltpu.VMEM((2, quarter, count, cells), F32),
            pltpu.VMEM((quarter, count, cells), F32),
            pltpu.VMEM((quarter, 2 * count, cells), BF16),
            pltpu.VMEM((quarter, nb, own, cells), F32),
            pltpu.VMEM((2, quarter, own, cells // 2), F32),
            pltpu.VMEM((5, most, count // 2, 128), F32),
            dma((quarter,)),
            dma((2,)),
            dma((8,)),
            dma((8,)),
            dma((2, planes)),
            dma((2, planes)),
            dma((planes,)),
            dma((planes,)),
            dma((2, quarter)),
            dma((2, quarter)),
            dma((2, quarter)),
            dma((2, quarter)),
            dma((5, most)),
            dma((5, most)),
            *[dma((2, quarter))] * 6,
        ],
        compiler_params=pltpu.CompilerParams(
            collective_id=0, has_side_effects=True, vmem_limit_bytes=67000000
        ),
    )(block_x, prior_x, potential)
    return out.transpose(1, 0, 2)


def solution(mesh):
    sizes = tuple(mesh.shape[a] for a in ("gx", "gy", "band"))
    in_specs = (P("band", "gx", "gy"), P("band", "gx", "gy"), P("gx", "gy"))
    out_specs = P("band", "gx", "gy")
    return jax.shard_map(
        functools.partial(shards, sizes), mesh=mesh, in_specs=in_specs, out_specs=out_specs, check_vma=False
    )
```

```python
import functools

import jax
import jax.numpy as jnp
from jax import lax
from jax.experimental import pallas as pl
from jax.experimental.pallas import tpu as pltpu
from jax.sharding import PartitionSpec as P

NZ = 192
WIDTH = 4 * NZ
CHUNK = 2 * NZ
WIDE = 2 * CHUNK
F32 = jnp.float32
BF16 = jnp.bfloat16
MESH = pl.DeviceIdType.MESH

coeffs = (-205.0 / 72.0, 8.0 / 5.0, -1.0 / 5.0, 8.0 / 315.0, -1.0 / 560.0)


def halves(value):
    high = value.astype(BF16)
    low = (value - high.astype(F32)).astype(BF16)
    return jnp.concatenate([high, low], axis=0)


def dot(left, right):
    return jnp.dot(left, right, preferred_element_type=F32)


def dot_nt(left, right):
    return lax.dot_general(left, right, (((1,), (1,)), ((), ())), preferred_element_type=F32)


def remote(src, dst, send, recv, axis, peer):
    return pltpu.make_async_remote_copy(
        src_ref=src, dst_ref=dst, send_sem=send, recv_sem=recv, device_id={axis: peer}, device_id_type=MESH
    )


def stacked_halves(value):
    high = value.astype(BF16).astype(F32)
    return jnp.concatenate([high, value - high], axis=0).astype(BF16)


def pack(value, parts):
    rows, lanes = value.shape[0] // parts, value.shape[1] // parts
    group = lax.broadcasted_iota(jnp.int32, (rows, value.shape[1]), 1) // lanes
    packed = value[:rows]
    for k in range(1, parts):
        packed = jnp.where(group == k, value[k * rows : (k + 1) * rows], packed)
    return packed


def unpack(packed, parts):
    width = packed.shape[1]
    moved = [packed] + [pltpu.roll(packed, width - k * (width // parts), axis=1) for k in range(1, parts)]
    return jnp.concatenate(moved, axis=0)


def inverse_factor(gram):
    count = gram.shape[0]
    row = lax.broadcasted_iota(jnp.int32, gram.shape, 0)
    lane = lax.broadcasted_iota(jnp.int32, gram.shape, 1)
    table = jnp.where(lane < count, gram, jnp.where(lane - count == row, 1.0, 0.0))
    for k in range(count - 1):
        pivot = table[k : k + 1, :]
        factor = table[:, k : k + 1] / table[k : k + 1, k : k + 1]
        table = table - jnp.where(row > k, factor, 0.0) * pivot
    diagonal = jnp.sum(jnp.where(lane == row, table, 0.0), axis=1, keepdims=True)
    inverse = jnp.where((lane >= count) & (lane < 2 * count), table * (1.0 / jnp.sqrt(diagonal)), 0.0)
    return inverse + pltpu.roll(inverse, gram.shape[1] - count, axis=1)


def kernel(
    sizes, ncells, block, prior, potential, out,
    grid, phi, staged, stacked, product, opposite, sides, opposite_in, sides_in, projected, pieces, result, passing, slots,
    local_sem, stage_sem, halo_send, halo_recv, ring_send, ring_recv, relay_send, relay_recv,
    opp_send, opp_recv, side_send, side_recv, sum_send, sum_recv, back_send, back_recv,
    hop_send, hop_recv, last_send, last_recv,
):
    nx, ny, nb = sizes
    gx, gy, band = lax.axis_index("gx"), lax.axis_index("gy"), lax.axis_index("band")
    planes, own, cells = block.shape
    quarter = planes // nb
    count = nb * own
    right, left, across = lax.rem(band + 1, nb), lax.rem(band + nb - 1, nb), lax.rem(band + 2, nb)

    fill = pltpu.make_async_copy(block, grid.at[pl.ds(4, planes), :, pl.ds(WIDTH, cells)], local_sem.at[0])
    fill.start()

    def stage(x, slot):
        return pltpu.make_async_copy(prior.at[x], staged.at[slot], stage_sem.at[slot])

    stage(4, 0).start()
    stage(5, 1).start()

    barrier = pltpu.get_barrier_semaphore()
    for axis, me, n in (("gx", gx, nx), ("gy", gy, ny), ("band", band, nb)):
        for k in range(1, n):
            pl.semaphore_signal(barrier, inc=1, device_id={axis: lax.rem(me + k, n)}, device_id_type=MESH)
    pl.semaphore_wait(barrier, nx + ny + nb - 3)

    middle = pl.ds(WIDTH, cells)
    low, high = pl.ds(0, WIDTH), pl.ds(cells - WIDTH, WIDTH)
    above = pl.ds(WIDTH + cells, WIDTH)

    def y_halos(at, first, size):
        here, there = pl.ds(first, size), pl.ds(4 + first, size)
        return (
            (at, "gy", gy, ny, 1, block.at[here, :, high], grid.at[there, :, low]),
            (at + 1, "gy", gy, ny, -1, block.at[here, :, low], grid.at[there, :, above]),
        )

    halos = (
        *y_halos(0, 4, planes - 8),
        (2, "gx", gx, nx, 1, block.at[pl.ds(planes - 4, 4)], grid.at[pl.ds(0, 4), :, middle]),
        (3, "gx", gx, nx, -1, block.at[pl.ds(0, 4)], grid.at[pl.ds(planes + 4, 4), :, middle]),
        *y_halos(4, planes - 4, 4),
        *y_halos(6, 0, 4),
    )

    def halo(at, axis, me, n, step, src, dst):
        copy = remote(src, dst, halo_send.at[at], halo_recv.at[at], axis, lax.rem(me + step + n, n))
        sends, receives = (me < n - 1, me > 0) if step == 1 else (me > 0, me < n - 1)
        return copy, sends, receives, dst

    def depart(entries):
        for entry in entries:
            copy, sends, receives, dst = halo(*entry)
            pl.when(sends)(copy.start)

    depart(halos[:4])
    for entry in halos:
        copy, sends, receives, dst = halo(*entry)

        @pl.when(jnp.logical_not(receives))
        def _(dst=dst):
            dst[...] = jnp.zeros(dst.shape, F32)

    fill.wait()

    def arrive(entries):
        for entry in entries:
            copy, sends, receives, dst = halo(*entry)
            pl.when(receives)(copy.wait_recv)
            pl.when(sends)(copy.wait_send)

    depth = lax.rem(lax.broadcasted_iota(jnp.int32, (own, CHUNK), 1), NZ)
    ups = [jnp.where(depth < NZ - m, coeffs[m], 0.0).astype(F32) for m in range(1, 5)]
    downs = [jnp.where(depth >= m, coeffs[m], 0.0).astype(F32) for m in range(1, 5)]

    def to_right(x):
        return remote(phi.at[x, 0], phi.at[x, 1], ring_send.at[0, x], ring_recv.at[0, x], "band", right)

    def to_left(x):
        return remote(phi.at[x, 0], phi.at[x, 2], ring_send.at[1, x], ring_recv.at[1, x], "band", left)

    def place(i):
        return lax.rem(i + 4, planes)

    def hamiltonian(i, carry):
        x = place(i)
        for start in range(0, cells, CHUNK):
            s = WIDTH + start
            center = grid[x + 4, :, pl.ds(s, CHUNK)]
            total = 3.0 * coeffs[0] * center
            for m in range(1, 5):
                total = total + coeffs[m] * (
                    grid[x + 4 + m, :, pl.ds(s, CHUNK)] + grid[x + 4 - m, :, pl.ds(s, CHUNK)]
                )
            for m in (2, 4):
                total = total + coeffs[m] * (
                    grid[x + 4, :, pl.ds(s + m * NZ, CHUNK)] + grid[x + 4, :, pl.ds(s - m * NZ, CHUNK)]
                )
            odd = None
            for m in (1, 3):
                term = coeffs[m] * (
                    grid[x + 4, :, pl.ds(s + m * NZ - 64, CHUNK + 128)]
                    + grid[x + 4, :, pl.ds(s - m * NZ - 64, CHUNK + 128)]
                )
                odd = term if odd is None else odd + term
            total = total + pltpu.roll(odd, CHUNK + 64, axis=1)[:, :CHUNK]
            for m in range(1, 5):
                total = total + ups[m - 1] * pltpu.roll(center, CHUNK - m, axis=1)
                total = total + downs[m - 1] * pltpu.roll(center, m, axis=1)
            weight = potential[pl.ds(x, 1), pl.ds(start, CHUNK)]
            phi[x, 0, :, pl.ds(start, CHUNK)] = weight * center - 2.0 * total
        to_right(x).start()
        to_left(x).start()
        return carry

    arrive(halos[:2])
    depart(halos[4:])
    lax.fori_loop(0, planes - 8, hamiltonian, 0)
    arrive(halos[2:])
    lax.fori_loop(planes - 8, planes, hamiltonian, 0)

    def relay_right(x):
        return remote(phi.at[x, 1], phi.at[x, 3], relay_send.at[x], relay_recv.at[x], "band", right)

    def relay_left(x):
        return remote(phi.at[x, 2], phi.at[x, 3], relay_send.at[x], relay_recv.at[x], "band", left)

    relays = (relay_right, relay_left)
    product[...] = jnp.zeros_like(product)
    pairs = planes // 2
    near = 3 * own
    early_rows, late_rows, gram_rows = pl.ds(0, 2 * near), pl.ds(2 * near, 2 * own), pl.ds(2 * count, 2 * count)

    def gather_near(i, carry):
        x, slot = place(i), lax.rem(i, 2)
        stage(x, slot).wait()
        stacked[x] = halves(staged[slot])

        @pl.when(i < planes - 2)
        def _():
            stage(place(i + 2), slot).start()

        to_right(x).wait_recv()
        to_left(x).wait_recv()
        product[early_rows, :] += dot_nt(stacked_halves(phi[x, 0:3].reshape(near, cells)), stacked[x])
        return carry

    def start_relays(i, carry):
        for k in range(2):
            relays[k](place(2 * i + k)).start()
        return carry

    def gather_far(i, carry):
        for k in range(2):
            x = place(2 * i + k)
            relays[k](x).wait()
            to_right(x).wait_send()
            to_left(x).wait_send()
            product[late_rows, :] += dot_nt(stacked_halves(phi[x, 3]), stacked[x])
        return carry

    def sum_start(at, axis, me, n, value):
        rows = pl.ds(0, value.shape[0])
        slots[at, me, rows] = value
        for k in range(1, n):
            sum_copy(at, axis, me, n, rows, k).start()

    def sum_copy(at, axis, me, n, rows, k):
        return remote(
            slots.at[at, me, rows], slots.at[at, me, rows],
            sum_send.at[at, k - 1], sum_recv.at[at, k - 1], axis, lax.rem(me + k, n),
        )

    def sum_finish(at, axis, me, n, size):
        rows = pl.ds(0, size)
        for k in range(1, n):
            sum_copy(at, axis, me, n, rows, k).wait()
        value = slots[at, 0, rows]
        for k in range(1, n):
            value = value + slots[at, k, rows]
        return value

    lax.fori_loop(0, planes - 2, gather_near, 0)
    lax.fori_loop(0, pairs - 1, start_relays, 0)
    lax.fori_loop(planes - 2, planes, gather_near, 0)
    start_relays(pairs - 1, 0)

    scale = 1.0 / ncells
    lane = lax.broadcasted_iota(jnp.int32, (own, 128), 1)
    folded = product[pl.ds(0, near), :] + product[pl.ds(near, near), :]
    folded = folded + pltpu.roll(folded, 64, axis=1)
    first = jnp.where(lane < 64, folded[:own], folded[own : 2 * own])
    sum_start(0, "gx", gx, nx, jnp.concatenate([first, folded[2 * own :]], axis=0))
    gather_far(0, 0)
    sum_start(1, "gy", gy, ny, sum_finish(0, "gx", gx, nx, 2 * own))
    gather_far(1, 0)
    packed = sum_finish(1, "gy", gy, ny, 2 * own) * scale
    first, third = packed[:own], packed[own:]
    other = pltpu.roll(first, 64, axis=1)
    near_weights = stacked_halves(
        jnp.concatenate([jnp.where(lane < 64, first, other), jnp.where(lane < 64, other, first), third], axis=0)
    )

    def removed_near(x, store):
        for start in range(0, cells, WIDE):
            both = dot(near_weights, stacked[x, :, pl.ds(start, WIDE)])
            store(pl.ds(start, WIDE), (both[:near] + both[near:]).reshape(3, own, WIDE))

    def across_copy(side, p, j):
        return remote(
            opposite.at[p, ((2, 0), (1, 3))[side][j]], opposite_in.at[side, p, j],
            opp_send.at[side, p, j], opp_recv.at[side, p, j], "band", (right, left)[side],
        )

    def side_copy(side, p, r):
        return remote(
            sides.at[side, p, r], sides_in.at[side, p, ((1, 3, 0, 2), (2, 0, 3, 1))[side][r]],
            side_send.at[side, p, r], side_recv.at[side, p, ((1, 3, 0, 2), (2, 0, 3, 1))[side][r]],
            "band", (right, left)[side],
        )

    def send_across(p, carry):
        def store(at, value):
            opposite[p, 0:3, :, at] = value

        removed_near(across * quarter + p, store)
        for side, j in ((0, 0), (0, 1), (1, 0)):
            across_copy(side, p, j).start()
        return carry

    def send_direct(p, carry):
        for side in range(2):

            def store(at, value, side=side):
                sides[side, p, 0:3, :, at] = value

            removed_near((right, left)[side] * quarter + p, store)
            side_copy(side, p, 2).start()
        return carry

    def add_and_send(side, p, j):
        across_copy(side, p, j).wait()
        sides[side, p, j] += opposite_in[side, p, j]
        side_copy(side, p, j).start()

    def relay_sums(p, carry):
        for side, j in ((1, 0), (0, 0), (0, 1)):
            add_and_send(side, p, j)
        return carry

    lax.fori_loop(0, quarter, send_across, 0)
    lax.fori_loop(0, quarter, send_direct, 0)
    lax.fori_loop(2, pairs, gather_far, 0)
    folded = product[pl.ds(2 * near, own), :] + product[pl.ds(2 * near + own, own), :]
    sum_start(5, "gx", gx, nx, folded + pltpu.roll(folded, 64, axis=1))
    lax.fori_loop(0, quarter - 1, relay_sums, 0)
    sum_start(6, "gy", gy, ny, sum_finish(5, "gx", gx, nx, own))
    lax.fori_loop(quarter - 1, quarter, relay_sums, 0)
    far_weights = stacked_halves(sum_finish(6, "gy", gy, ny, own) * scale)

    def removed_far(x, store):
        for start in range(0, cells, WIDE):
            both = dot(far_weights, stacked[x, :, pl.ds(start, WIDE)])
            store(pl.ds(start, WIDE), both[:own] + both[own:])

    def send_across_far(p, carry):
        def store(at, value):
            opposite[p, 3, :, at] = value

        removed_far(across * quarter + p, store)
        across_copy(1, p, 1).start()
        return carry

    def send_direct_far(p, carry):
        for side in range(2):

            def store(at, value, side=side):
                sides[side, p, 3, :, at] = value

            removed_far((right, left)[side] * quarter + p, store)
            side_copy(side, p, 3).start()
        return carry

    def relay_sums_far(p, carry):
        add_and_send(1, p, 1)
        return carry

    def own_part(p, carry):
        x = band * quarter + p

        def store(at, value):
            projected[p, 0:3, :, at] = phi[x, 0:3, :, at] - value

        def store_far(at, value):
            projected[p, 3, :, at] = phi[x, 3, :, at] - value

        removed_near(x, store)
        removed_far(x, store_far)
        return carry

    lax.fori_loop(0, quarter, send_across_far, 0)
    lax.fori_loop(0, quarter, send_direct_far, 0)
    lax.fori_loop(0, quarter, relay_sums_far, 0)
    lax.fori_loop(0, quarter, own_part, 0)
    slabs = (band, left, right, across)

    def inner_products(p, carry):
        for side in range(2):
            for r in range(4):
                side_copy(side, p, r).wait_send()
                side_copy(side, p, r).wait_recv()
        for r in range(4):
            result[p, slabs[r]] = projected[p, r] - (sides_in[0, p, r] + sides_in[1, p, r])
        for start in range(0, cells, WIDE):
            at = pl.ds(start, WIDE)
            pieces[p, :, at] = halves(result[p, :, :, at].reshape(count, WIDE))
        both = pieces[p]
        product[gram_rows, :] += dot_nt(both, jnp.concatenate([both, both], axis=0))
        return carry

    lax.fori_loop(0, quarter, inner_products, 0)

    folded = product[pl.ds(2 * count, count), :] + product[pl.ds(3 * count, count), :]
    folded = folded + pltpu.roll(folded, count, axis=1)
    packed = pack(folded, 4)
    for entry in ((2, "gx", gx, nx), (3, "gy", gy, ny), (4, "band", band, nb)):
        sum_start(*entry, packed)
        packed = sum_finish(*entry, own)
    inverse = halves(inverse_factor(unpack(packed, 4) * scale))[:, : 2 * count]

    split = cells // 2

    def back(p, side):
        peer = (right, left)[side]
        return remote(
            result.at[p, peer], out.at[band * quarter + p], back_send.at[side, p], back_recv.at[side, p], "band", peer
        )

    def first_hop(p, side):
        part = pl.ds(side * split, split)
        return remote(
            result.at[p, across, :, part], passing.at[side, p],
            hop_send.at[side, p], hop_recv.at[side, p], "band", (right, left)[side],
        )

    def second_hop(p, side):
        part = pl.ds(side * split, split)
        return remote(
            passing.at[side, p], out.at[(left, right)[side] * quarter + p, :, part],
            last_send.at[side, p], last_recv.at[side, p], "band", (right, left)[side],
        )

    def keep(p):
        return pltpu.make_async_copy(result.at[p, band], out.at[band * quarter + p], local_sem.at[p])

    def finish(p, carry):
        for start in range(0, cells, WIDE):
            at = pl.ds(start, WIDE)
            both = dot(inverse, pieces[p, :, at])
            result[p, :, :, at] = (both[:count] + both[count:]).reshape(nb, own, WIDE)
        for side in range(2):
            first_hop(p, side).start()
        for side in range(2):
            back(p, side).start()
        keep(p).start()
        return carry

    lax.fori_loop(0, quarter, finish, 0)

    def forward(p, carry):
        for side in range(2):
            first_hop(p, side).wait()
            second_hop(p, side).start()
        return carry

    lax.fori_loop(0, quarter, forward, 0)

    def drain(p, carry):
        for side in range(2):
            back(p, side).wait()
            second_hop(p, side).wait()
        keep(p).wait()
        return carry

    lax.fori_loop(0, quarter, drain, 0)


def shards(sizes, block, prior, potential):
    nx, ny, nb = sizes
    block_x, prior_x = block.transpose(1, 0, 2), prior.transpose(1, 0, 2)
    planes, own, cells = block_x.shape
    priors, count, quarter = prior_x.shape[1], own * nb, planes // nb
    ncells = planes * nx * cells * ny
    dma = pltpu.SemaphoreType.DMA
    most = max(sizes)
    out = pl.pallas_call(
        functools.partial(kernel, sizes, ncells),
        out_shape=jax.ShapeDtypeStruct(block_x.shape, F32),
        in_specs=[
            pl.BlockSpec(memory_space=pl.ANY),
            pl.BlockSpec(memory_space=pl.ANY),
            pl.BlockSpec(memory_space=pltpu.VMEM),
        ],
        out_specs=pl.BlockSpec(memory_space=pl.ANY),
        scratch_shapes=[
            pltpu.VMEM((planes + 8, own, cells + 2 * WIDTH), F32),
            pltpu.VMEM((planes, nb, own, cells), F32),
            pltpu.VMEM((2, priors, cells), F32),
            pltpu.VMEM((planes, 2 * priors, cells), BF16),
            pltpu.VMEM((4 * count, 128), F32),
            pltpu.VMEM((quarter, nb, own, cells), F32),
            pltpu.VMEM((2, quarter, nb, own, cells), F32),
            pltpu.VMEM((2, quarter, 2, own, cells), F32),
            pltpu.VMEM((2, quarter, nb, own, cells), F32),
            pltpu.VMEM((quarter, nb, own, cells), F32),
            pltpu.VMEM((quarter, 2 * count, cells), BF16),
            pltpu.VMEM((quarter, nb, own, cells), F32),
            pltpu.VMEM((2, quarter, own, cells // 2), F32),
            pltpu.VMEM((7, most, 2 * own, 128), F32),
            dma((quarter,)),
            dma((2,)),
            dma((8,)),
            dma((8,)),
            dma((2, planes)),
            dma((2, planes)),
            dma((planes,)),
            dma((planes,)),
            dma((2, quarter, 2)),
            dma((2, quarter, 2)),
            dma((2, quarter, nb)),
            dma((2, quarter, nb)),
            dma((7, most)),
            dma((7, most)),
            *[dma((2, quarter))] * 6,
        ],
        compiler_params=pltpu.CompilerParams(
            collective_id=0, has_side_effects=True, vmem_limit_bytes=67000000
        ),
    )(block_x, prior_x, potential)
    return out.transpose(1, 0, 2)


def solution(mesh):
    sizes = tuple(mesh.shape[a] for a in ("gx", "gy", "band"))
    in_specs = (P("band", "gx", "gy"), P("band", "gx", "gy"), P("gx", "gy"))
    out_specs = P("band", "gx", "gy")
    return jax.shard_map(
        functools.partial(shards, sizes), mesh=mesh, in_specs=in_specs, out_specs=out_specs, check_vma=False
    )
```

```python
import functools

import jax
import jax.numpy as jnp
from jax import lax
from jax.experimental import pallas as pl
from jax.experimental.pallas import tpu as pltpu
from jax.sharding import PartitionSpec as P

NZ = 192
WIDTH = 4 * NZ
CHUNK = 2 * NZ
WIDE = 2 * CHUNK
F32 = jnp.float32
BF16 = jnp.bfloat16
MESH = pl.DeviceIdType.MESH

coeffs = (-205.0 / 72.0, 8.0 / 5.0, -1.0 / 5.0, 8.0 / 315.0, -1.0 / 560.0)


def halves(value):
    high = value.astype(BF16)
    low = (value - high.astype(F32)).astype(BF16)
    return jnp.concatenate([high, low], axis=0)


def dot(left, right):
    return jnp.dot(left, right, preferred_element_type=F32)


def dot_nt(left, right):
    return lax.dot_general(left, right, (((1,), (1,)), ((), ())), preferred_element_type=F32)


def remote(src, dst, send, recv, axis, peer):
    return pltpu.make_async_remote_copy(
        src_ref=src, dst_ref=dst, send_sem=send, recv_sem=recv, device_id={axis: peer}, device_id_type=MESH
    )


def stacked_halves(value):
    high = value.astype(BF16).astype(F32)
    return jnp.concatenate([high, value - high], axis=0).astype(BF16)


def pack(value, parts):
    rows, lanes = value.shape[0] // parts, value.shape[1] // parts
    group = lax.broadcasted_iota(jnp.int32, (rows, value.shape[1]), 1) // lanes
    packed = value[:rows]
    for k in range(1, parts):
        packed = jnp.where(group == k, value[k * rows : (k + 1) * rows], packed)
    return packed


def unpack(packed, parts):
    width = packed.shape[1]
    moved = [packed] + [pltpu.roll(packed, width - k * (width // parts), axis=1) for k in range(1, parts)]
    return jnp.concatenate(moved, axis=0)


def inverse_factor(gram):
    count = gram.shape[0]
    row = lax.broadcasted_iota(jnp.int32, gram.shape, 0)
    lane = lax.broadcasted_iota(jnp.int32, gram.shape, 1)
    table = jnp.where(lane < count, gram, jnp.where(lane - count == row, 1.0, 0.0))
    for k in range(count - 1):
        pivot = table[k : k + 1, :]
        factor = table[:, k : k + 1] / table[k : k + 1, k : k + 1]
        table = table - jnp.where(row > k, factor, 0.0) * pivot
    diagonal = jnp.sum(jnp.where(lane == row, table, 0.0), axis=1, keepdims=True)
    inverse = jnp.where((lane >= count) & (lane < 2 * count), table * (1.0 / jnp.sqrt(diagonal)), 0.0)
    return inverse + pltpu.roll(inverse, gram.shape[1] - count, axis=1)


def kernel(
    sizes, ncells, block, prior, weights, out,
    potential, grid, phi, staged, stacked, product, opposite, sides, opposite_in, sides_in, projected, pieces, result, passing, slots,
    local_sem, stage_sem, halo_send, halo_recv, ring_send, ring_recv, relay_send, relay_recv,
    opp_send, opp_recv, side_send, side_recv, sum_send, sum_recv, back_send, back_recv,
    hop_send, hop_recv, last_send, last_recv,
):
    nx, ny, nb = sizes
    gx, gy, band = lax.axis_index("gx"), lax.axis_index("gy"), lax.axis_index("band")
    planes, own, cells = block.shape
    quarter = planes // nb
    count = nb * own
    right, left, across = lax.rem(band + 1, nb), lax.rem(band + nb - 1, nb), lax.rem(band + 2, nb)

    barrier = pltpu.get_barrier_semaphore()
    for axis, me, n in (("gx", gx, nx), ("gy", gy, ny), ("band", band, nb)):
        for k in range(1, n):
            pl.semaphore_signal(barrier, inc=1, device_id={axis: lax.rem(me + k, n)}, device_id_type=MESH)

    fill = pltpu.make_async_copy(block, grid.at[pl.ds(4, planes), :, pl.ds(WIDTH, cells)], local_sem.at[0])
    fill.start()
    fill_weights = pltpu.make_async_copy(weights, potential, local_sem.at[1])
    fill_weights.start()

    def stage(x, slot):
        return pltpu.make_async_copy(prior.at[x], staged.at[slot], stage_sem.at[slot])

    stage(4, 0).start()
    stage(5, 1).start()

    middle = pl.ds(WIDTH, cells)
    low, high = pl.ds(0, WIDTH), pl.ds(cells - WIDTH, WIDTH)
    above = pl.ds(WIDTH + cells, WIDTH)

    def y_halos(at, first, size):
        here, there = pl.ds(first, size), pl.ds(4 + first, size)
        return (
            (at, "gy", gy, ny, 1, block.at[here, :, high], grid.at[there, :, low]),
            (at + 1, "gy", gy, ny, -1, block.at[here, :, low], grid.at[there, :, above]),
        )

    halos = (
        *y_halos(0, 4, planes - 8),
        (2, "gx", gx, nx, 1, block.at[pl.ds(planes - 4, 4)], grid.at[pl.ds(0, 4), :, middle]),
        (3, "gx", gx, nx, -1, block.at[pl.ds(0, 4)], grid.at[pl.ds(planes + 4, 4), :, middle]),
        *y_halos(4, planes - 4, 4),
        *y_halos(6, 0, 4),
    )

    def halo(at, axis, me, n, step, src, dst):
        copy = remote(src, dst, halo_send.at[at], halo_recv.at[at], axis, lax.rem(me + step + n, n))
        sends, receives = (me < n - 1, me > 0) if step == 1 else (me > 0, me < n - 1)
        return copy, sends, receives, dst

    def depart(entries):
        for entry in entries:
            copy, sends, receives, dst = halo(*entry)
            pl.when(sends)(copy.start)

    for entry in halos:
        copy, sends, receives, dst = halo(*entry)

        @pl.when(jnp.logical_not(receives))
        def _(dst=dst):
            dst[...] = jnp.zeros(dst.shape, F32)

    def arrive(entries):
        for entry in entries:
            copy, sends, receives, dst = halo(*entry)
            pl.when(receives)(copy.wait_recv)
            pl.when(sends)(copy.wait_send)

    depth = lax.rem(lax.broadcasted_iota(jnp.int32, (own, CHUNK), 1), NZ)
    ups = [jnp.where(depth < NZ - m, coeffs[m], 0.0).astype(F32) for m in range(1, 5)]
    downs = [jnp.where(depth >= m, coeffs[m], 0.0).astype(F32) for m in range(1, 5)]

    def to_right(x):
        return remote(phi.at[x, 0], phi.at[x, 1], ring_send.at[0, x], ring_recv.at[0, x], "band", right)

    def to_left(x):
        return remote(phi.at[x, 0], phi.at[x, 2], ring_send.at[1, x], ring_recv.at[1, x], "band", left)

    def place(i):
        return lax.rem(i + 4, planes)

    def hamiltonian(x, starts):
        for start in starts:
            s = WIDTH + start
            center = grid[x + 4, :, pl.ds(s, CHUNK)]
            total = 3.0 * coeffs[0] * center
            for m in range(1, 5):
                total = total + coeffs[m] * (
                    grid[x + 4 + m, :, pl.ds(s, CHUNK)] + grid[x + 4 - m, :, pl.ds(s, CHUNK)]
                )
            for m in (2, 4):
                total = total + coeffs[m] * (
                    grid[x + 4, :, pl.ds(s + m * NZ, CHUNK)] + grid[x + 4, :, pl.ds(s - m * NZ, CHUNK)]
                )
            odd = None
            for m in (1, 3):
                term = coeffs[m] * (
                    grid[x + 4, :, pl.ds(s + m * NZ - 64, CHUNK + 128)]
                    + grid[x + 4, :, pl.ds(s - m * NZ - 64, CHUNK + 128)]
                )
                odd = term if odd is None else odd + term
            total = total + pltpu.roll(odd, CHUNK + 64, axis=1)[:, :CHUNK]
            for m in range(1, 5):
                total = total + ups[m - 1] * pltpu.roll(center, CHUNK - m, axis=1)
                total = total + downs[m - 1] * pltpu.roll(center, m, axis=1)
            weight = potential[pl.ds(x, 1), pl.ds(start, CHUNK)]
            phi[x, 0, :, pl.ds(start, CHUNK)] = weight * center - 2.0 * total

    def send_part(x, first, size):
        part = pl.ds(first, size)
        for side in range(2):
            remote(
                phi.at[x, 0, :, part], phi.at[x, 1 + side, :, part],
                ring_send.at[side, x], ring_recv.at[side, x], "band", (right, left)[side],
            ).start()

    def inside(i, carry):
        hamiltonian(place(i), range(WIDTH, cells - WIDTH, CHUNK))
        return carry

    def send_inside(i, carry):
        send_part(place(i), WIDTH, cells - 2 * WIDTH)
        return carry

    def edges(i, carry):
        x = place(i)
        for first in (0, cells - WIDTH):
            hamiltonian(x, range(first, first + WIDTH, CHUNK))
        for first in (0, cells - WIDTH):
            send_part(x, first, WIDTH)
        return carry

    def whole(i, carry):
        x = place(i)
        hamiltonian(x, range(0, cells, CHUNK))
        to_right(x).start()
        to_left(x).start()
        return carry

    fill.wait()
    fill_weights.wait()
    lax.fori_loop(0, planes - 8, inside, 0)
    pl.semaphore_wait(barrier, nx + ny + nb - 3)
    depart(halos[:4])
    lax.fori_loop(0, planes - 8, send_inside, 0)
    arrive(halos[:2])
    depart(halos[4:])
    lax.fori_loop(0, planes - 8, edges, 0)
    arrive(halos[2:])
    lax.fori_loop(planes - 8, planes, whole, 0)

    def relay_right(x):
        return remote(phi.at[x, 1], phi.at[x, 3], relay_send.at[x], relay_recv.at[x], "band", right)

    def relay_left(x):
        return remote(phi.at[x, 2], phi.at[x, 3], relay_send.at[x], relay_recv.at[x], "band", left)

    relays = (relay_right, relay_left)
    product[...] = jnp.zeros_like(product)
    pairs = planes // 2
    near = 3 * own
    early_rows, late_rows, gram_rows = pl.ds(0, 2 * near), pl.ds(2 * near, 2 * own), pl.ds(2 * count, 2 * count)

    def gather_near(i, carry):
        x, slot = place(i), lax.rem(i, 2)
        stage(x, slot).wait()
        stacked[x] = halves(staged[slot])

        @pl.when(i < planes - 2)
        def _():
            stage(place(i + 2), slot).start()

        to_right(x).wait_recv()
        to_left(x).wait_recv()
        product[early_rows, :] += dot_nt(stacked_halves(phi[x, 0:3].reshape(near, cells)), stacked[x])
        return carry

    def start_relays(i, carry):
        for k in range(2):
            relays[k](place(2 * i + k)).start()
        return carry

    def gather_far(i, carry):
        for k in range(2):
            x = place(2 * i + k)
            relays[k](x).wait()
            to_right(x).wait_send()
            to_left(x).wait_send()
            product[late_rows, :] += dot_nt(stacked_halves(phi[x, 3]), stacked[x])
        return carry

    def sum_start(at, axis, me, n, value):
        rows = pl.ds(0, value.shape[0])
        slots[at, me, rows] = value
        for k in range(1, n):
            sum_copy(at, axis, me, n, rows, k).start()

    def sum_copy(at, axis, me, n, rows, k):
        return remote(
            slots.at[at, me, rows], slots.at[at, me, rows],
            sum_send.at[at, k - 1], sum_recv.at[at, k - 1], axis, lax.rem(me + k, n),
        )

    def sum_finish(at, axis, me, n, size):
        rows = pl.ds(0, size)
        for k in range(1, n):
            sum_copy(at, axis, me, n, rows, k).wait()
        value = slots[at, 0, rows]
        for k in range(1, n):
            value = value + slots[at, k, rows]
        return value

    lax.fori_loop(0, planes - 2, gather_near, 0)
    lax.fori_loop(0, pairs - 1, start_relays, 0)
    lax.fori_loop(planes - 2, planes, gather_near, 0)
    start_relays(pairs - 1, 0)

    scale = 1.0 / ncells
    lane = lax.broadcasted_iota(jnp.int32, (own, 128), 1)
    folded = product[pl.ds(0, near), :] + product[pl.ds(near, near), :]
    folded = folded + pltpu.roll(folded, 64, axis=1)
    first = jnp.where(lane < 64, folded[:own], folded[own : 2 * own])
    sum_start(0, "gx", gx, nx, jnp.concatenate([first, folded[2 * own :]], axis=0))
    gather_far(0, 0)
    sum_start(1, "gy", gy, ny, sum_finish(0, "gx", gx, nx, 2 * own))
    gather_far(1, 0)
    packed = sum_finish(1, "gy", gy, ny, 2 * own) * scale
    first, third = packed[:own], packed[own:]
    other = pltpu.roll(first, 64, axis=1)
    near_weights = stacked_halves(
        jnp.concatenate([jnp.where(lane < 64, first, other), jnp.where(lane < 64, other, first), third], axis=0)
    )

    def removed_near(x, store):
        for start in range(0, cells, WIDE):
            both = dot(near_weights, stacked[x, :, pl.ds(start, WIDE)])
            store(pl.ds(start, WIDE), (both[:near] + both[near:]).reshape(3, own, WIDE))

    def across_copy(side, p, j):
        return remote(
            opposite.at[p, ((2, 0), (1, 3))[side][j]], opposite_in.at[side, p, j],
            opp_send.at[side, p, j], opp_recv.at[side, p, j], "band", (right, left)[side],
        )

    def side_copy(side, p, r):
        return remote(
            sides.at[side, p, r], sides_in.at[side, p, ((1, 3, 0, 2), (2, 0, 3, 1))[side][r]],
            side_send.at[side, p, r], side_recv.at[side, p, ((1, 3, 0, 2), (2, 0, 3, 1))[side][r]],
            "band", (right, left)[side],
        )

    def send_across(p, carry):
        def store(at, value):
            opposite[p, 0:3, :, at] = value

        removed_near(across * quarter + p, store)
        for side, j in ((0, 0), (0, 1), (1, 0)):
            across_copy(side, p, j).start()
        return carry

    def send_direct(p, carry):
        for side in range(2):

            def store(at, value, side=side):
                sides[side, p, 0:3, :, at] = value

            removed_near((right, left)[side] * quarter + p, store)
            side_copy(side, p, 2).start()
        return carry

    def add_and_send(side, p, j):
        across_copy(side, p, j).wait()
        sides[side, p, j] += opposite_in[side, p, j]
        side_copy(side, p, j).start()

    def relay_sums(p, carry):
        for side, j in ((1, 0), (0, 0), (0, 1)):
            add_and_send(side, p, j)
        return carry

    lax.fori_loop(0, quarter, send_across, 0)
    lax.fori_loop(0, quarter, send_direct, 0)
    lax.fori_loop(2, pairs, gather_far, 0)
    folded = product[pl.ds(2 * near, own), :] + product[pl.ds(2 * near + own, own), :]
    sum_start(5, "gx", gx, nx, folded + pltpu.roll(folded, 64, axis=1))
    lax.fori_loop(0, quarter - 1, relay_sums, 0)
    sum_start(6, "gy", gy, ny, sum_finish(5, "gx", gx, nx, own))
    lax.fori_loop(quarter - 1, quarter, relay_sums, 0)
    far_weights = stacked_halves(sum_finish(6, "gy", gy, ny, own) * scale)

    def removed_far(x, store):
        for start in range(0, cells, WIDE):
            both = dot(far_weights, stacked[x, :, pl.ds(start, WIDE)])
            store(pl.ds(start, WIDE), both[:own] + both[own:])

    def send_across_far(p, carry):
        def store(at, value):
            opposite[p, 3, :, at] = value

        removed_far(across * quarter + p, store)
        across_copy(1, p, 1).start()
        return carry

    def send_direct_far(p, carry):
        for side in range(2):

            def store(at, value, side=side):
                sides[side, p, 3, :, at] = value

            removed_far((right, left)[side] * quarter + p, store)
            side_copy(side, p, 3).start()
        return carry

    def relay_sums_far(p, carry):
        add_and_send(1, p, 1)
        return carry

    def own_part(p, carry):
        x = band * quarter + p

        def store(at, value):
            projected[p, 0:3, :, at] = phi[x, 0:3, :, at] - value

        def store_far(at, value):
            projected[p, 3, :, at] = phi[x, 3, :, at] - value

        removed_near(x, store)
        removed_far(x, store_far)
        return carry

    lax.fori_loop(0, quarter, send_across_far, 0)
    lax.fori_loop(0, quarter, send_direct_far, 0)
    lax.fori_loop(0, quarter, relay_sums_far, 0)
    lax.fori_loop(0, quarter, own_part, 0)
    slabs = (band, left, right, across)

    def inner_products(p, carry):
        for side in range(2):
            for r in range(4):
                side_copy(side, p, r).wait_send()
                side_copy(side, p, r).wait_recv()
        for r in range(4):
            result[p, slabs[r]] = projected[p, r] - (sides_in[0, p, r] + sides_in[1, p, r])
        for start in range(0, cells, WIDE):
            at = pl.ds(start, WIDE)
            pieces[p, :, at] = halves(result[p, :, :, at].reshape(count, WIDE))
        both = pieces[p]
        product[gram_rows, :] += dot_nt(both, jnp.concatenate([both, both], axis=0))
        return carry

    lax.fori_loop(0, quarter, inner_products, 0)

    folded = product[pl.ds(2 * count, count), :] + product[pl.ds(3 * count, count), :]
    folded = folded + pltpu.roll(folded, count, axis=1)
    packed = pack(folded, 4)
    for entry in ((2, "gx", gx, nx), (3, "gy", gy, ny), (4, "band", band, nb)):
        sum_start(*entry, packed)
        packed = sum_finish(*entry, own)
    inverse = halves(inverse_factor(unpack(packed, 4) * scale))[:, : 2 * count]

    split = cells // 2

    def back(p, side):
        peer = (right, left)[side]
        return remote(
            result.at[p, peer], out.at[band * quarter + p], back_send.at[side, p], back_recv.at[side, p], "band", peer
        )

    def first_hop(p, side):
        part = pl.ds(side * split, split)
        return remote(
            result.at[p, across, :, part], passing.at[side, p],
            hop_send.at[side, p], hop_recv.at[side, p], "band", (right, left)[side],
        )

    def second_hop(p, side):
        part = pl.ds(side * split, split)
        return remote(
            passing.at[side, p], out.at[(left, right)[side] * quarter + p, :, part],
            last_send.at[side, p], last_recv.at[side, p], "band", (right, left)[side],
        )

    def keep(p):
        return pltpu.make_async_copy(result.at[p, band], out.at[band * quarter + p], local_sem.at[p])

    def finish(p, carry):
        for start in range(0, cells, WIDE):
            at = pl.ds(start, WIDE)
            both = dot(inverse, pieces[p, :, at])
            result[p, :, :, at] = (both[:count] + both[count:]).reshape(nb, own, WIDE)
        for side in range(2):
            first_hop(p, side).start()
        for side in range(2):
            back(p, side).start()
        keep(p).start()
        return carry

    lax.fori_loop(0, quarter, finish, 0)

    def forward(p, carry):
        for side in range(2):
            first_hop(p, side).wait()
            second_hop(p, side).start()
        return carry

    lax.fori_loop(0, quarter, forward, 0)

    def drain(p, carry):
        for side in range(2):
            back(p, side).wait()
            second_hop(p, side).wait()
        keep(p).wait()
        return carry

    lax.fori_loop(0, quarter, drain, 0)


def shards(sizes, block, prior, potential):
    nx, ny, nb = sizes
    block_x, prior_x = block.transpose(1, 0, 2), prior.transpose(1, 0, 2)
    planes, own, cells = block_x.shape
    priors, count, quarter = prior_x.shape[1], own * nb, planes // nb
    ncells = planes * nx * cells * ny
    dma = pltpu.SemaphoreType.DMA
    most = max(sizes)
    out = pl.pallas_call(
        functools.partial(kernel, sizes, ncells),
        out_shape=jax.ShapeDtypeStruct(block_x.shape, F32),
        in_specs=[
            pl.BlockSpec(memory_space=pltpu.HBM),
            pl.BlockSpec(memory_space=pltpu.HBM),
            pl.BlockSpec(memory_space=pltpu.HBM),
        ],
        out_specs=pl.BlockSpec(memory_space=pl.ANY),
        scratch_shapes=[
            pltpu.VMEM((planes, cells), F32),
            pltpu.VMEM((planes + 8, own, cells + 2 * WIDTH), F32),
            pltpu.VMEM((planes, nb, own, cells), F32),
            pltpu.VMEM((2, priors, cells), F32),
            pltpu.VMEM((planes, 2 * priors, cells), BF16),
            pltpu.VMEM((4 * count, 128), F32),
            pltpu.VMEM((quarter, nb, own, cells), F32),
            pltpu.VMEM((2, quarter, nb, own, cells), F32),
            pltpu.VMEM((2, quarter, 2, own, cells), F32),
            pltpu.VMEM((2, quarter, nb, own, cells), F32),
            pltpu.VMEM((quarter, nb, own, cells), F32),
            pltpu.VMEM((quarter, 2 * count, cells), BF16),
            pltpu.VMEM((quarter, nb, own, cells), F32),
            pltpu.VMEM((2, quarter, own, cells // 2), F32),
            pltpu.VMEM((7, most, 2 * own, 128), F32),
            dma((quarter,)),
            dma((2,)),
            dma((8,)),
            dma((8,)),
            dma((2, planes)),
            dma((2, planes)),
            dma((planes,)),
            dma((planes,)),
            dma((2, quarter, 2)),
            dma((2, quarter, 2)),
            dma((2, quarter, nb)),
            dma((2, quarter, nb)),
            dma((7, most)),
            dma((7, most)),
            *[dma((2, quarter))] * 6,
        ],
        compiler_params=pltpu.CompilerParams(
            collective_id=0, has_side_effects=True, vmem_limit_bytes=53000000
        ),
    )(block_x, prior_x, potential)
    return out.transpose(1, 0, 2)


def solution(mesh):
    sizes = tuple(mesh.shape[a] for a in ("gx", "gy", "band"))
    in_specs = (P("band", "gx", "gy"), P("band", "gx", "gy"), P("gx", "gy"))
    out_specs = P("band", "gx", "gy")
    return jax.shard_map(
        functools.partial(shards, sizes), mesh=mesh, in_specs=in_specs, out_specs=out_specs, check_vma=False
    )
```

```python
import functools

import jax
import jax.numpy as jnp
from jax import lax
from jax.experimental import pallas as pl
from jax.experimental.pallas import tpu as pltpu
from jax.sharding import PartitionSpec as P

NZ = 192
WIDTH = 4 * NZ
CHUNK = 2 * NZ
WIDE = 2 * CHUNK
F32 = jnp.float32
BF16 = jnp.bfloat16
MESH = pl.DeviceIdType.MESH

coeffs = (-205.0 / 72.0, 8.0 / 5.0, -1.0 / 5.0, 8.0 / 315.0, -1.0 / 560.0)


def halves(value):
    high = value.astype(BF16)
    low = (value - high.astype(F32)).astype(BF16)
    return jnp.concatenate([high, low], axis=0)


def dot(left, right):
    return jnp.dot(left, right, preferred_element_type=F32)


def dot_nt(left, right):
    return lax.dot_general(left, right, (((1,), (1,)), ((), ())), preferred_element_type=F32)


def remote(src, dst, send, recv, axis, peer):
    return pltpu.make_async_remote_copy(
        src_ref=src, dst_ref=dst, send_sem=send, recv_sem=recv, device_id={axis: peer}, device_id_type=MESH
    )


def stacked_halves(value):
    high = value.astype(BF16).astype(F32)
    return jnp.concatenate([high, value - high], axis=0).astype(BF16)


def pack(value, parts):
    rows, lanes = value.shape[0] // parts, value.shape[1] // parts
    group = lax.broadcasted_iota(jnp.int32, (rows, value.shape[1]), 1) // lanes
    packed = value[:rows]
    for k in range(1, parts):
        packed = jnp.where(group == k, value[k * rows : (k + 1) * rows], packed)
    return packed


def unpack(packed, parts):
    width = packed.shape[1]
    moved = [packed] + [pltpu.roll(packed, width - k * (width // parts), axis=1) for k in range(1, parts)]
    return jnp.concatenate(moved, axis=0)


def inverse_factor(gram):
    count = gram.shape[0]
    row = lax.broadcasted_iota(jnp.int32, gram.shape, 0)
    lane = lax.broadcasted_iota(jnp.int32, gram.shape, 1)
    table = jnp.where(lane < count, gram, jnp.where(lane - count == row, 1.0, 0.0))
    for k in range(count - 1):
        pivot = table[k : k + 1, :]
        factor = table[:, k : k + 1] / table[k : k + 1, k : k + 1]
        table = table - jnp.where(row > k, factor, 0.0) * pivot
    diagonal = jnp.sum(jnp.where(lane == row, table, 0.0), axis=1, keepdims=True)
    inverse = jnp.where((lane >= count) & (lane < 2 * count), table * (1.0 / jnp.sqrt(diagonal)), 0.0)
    return inverse + pltpu.roll(inverse, gram.shape[1] - count, axis=1)


def kernel(
    sizes, ncells, block, prior, weights, out,
    potential, grid, phi, staged, stacked, product, opposite, sides, opposite_in, sides_in, projected, pieces, result, passing, slots,
    local_sem, stage_sem, halo_send, halo_recv, ring_send, ring_recv, relay_send, relay_recv,
    opp_send, opp_recv, side_send, side_recv, sum_send, sum_recv, back_send, back_recv,
    hop_send, hop_recv, last_send, last_recv,
):
    nx, ny, nb = sizes
    gx, gy, band = lax.axis_index("gx"), lax.axis_index("gy"), lax.axis_index("band")
    planes, own, cells = block.shape
    quarter = planes // nb
    count = nb * own
    right, left, across = lax.rem(band + 1, nb), lax.rem(band + nb - 1, nb), lax.rem(band + 2, nb)

    barrier = pltpu.get_barrier_semaphore()
    for axis, me, n in (("gx", gx, nx), ("gy", gy, ny), ("band", band, nb)):
        for k in range(1, n):
            pl.semaphore_signal(barrier, inc=1, device_id={axis: lax.rem(me + k, n)}, device_id_type=MESH)

    fill = pltpu.make_async_copy(block, grid.at[pl.ds(4, planes), :, pl.ds(WIDTH, cells)], local_sem.at[0])
    fill.start()
    fill_weights = pltpu.make_async_copy(weights, potential, local_sem.at[1])
    fill_weights.start()

    def stage(x, slot):
        return pltpu.make_async_copy(prior.at[x], staged.at[slot], stage_sem.at[slot])

    stage(4, 0).start()
    stage(5, 1).start()

    middle = pl.ds(WIDTH, cells)
    low, high = pl.ds(0, WIDTH), pl.ds(cells - WIDTH, WIDTH)
    above = pl.ds(WIDTH + cells, WIDTH)

    def y_halos(at, first, size):
        here, there = pl.ds(first, size), pl.ds(4 + first, size)
        return (
            (at, "gy", gy, ny, 1, block.at[here, :, high], grid.at[there, :, low]),
            (at + 1, "gy", gy, ny, -1, block.at[here, :, low], grid.at[there, :, above]),
        )

    halos = (
        *y_halos(0, 4, planes - 8),
        (2, "gx", gx, nx, 1, block.at[pl.ds(planes - 4, 4)], grid.at[pl.ds(0, 4), :, middle]),
        (3, "gx", gx, nx, -1, block.at[pl.ds(0, 4)], grid.at[pl.ds(planes + 4, 4), :, middle]),
        *y_halos(4, planes - 4, 4),
        *y_halos(6, 0, 4),
    )

    def halo(at, axis, me, n, step, src, dst):
        copy = remote(src, dst, halo_send.at[at], halo_recv.at[at], axis, lax.rem(me + step + n, n))
        sends, receives = (me < n - 1, me > 0) if step == 1 else (me > 0, me < n - 1)
        return copy, sends, receives, dst

    def depart(entries):
        for entry in entries:
            copy, sends, receives, dst = halo(*entry)
            pl.when(sends)(copy.start)

    for entry in halos:
        copy, sends, receives, dst = halo(*entry)

        @pl.when(jnp.logical_not(receives))
        def _(dst=dst):
            dst[...] = jnp.zeros(dst.shape, F32)

    def arrive(entries):
        for entry in entries:
            copy, sends, receives, dst = halo(*entry)
            pl.when(receives)(copy.wait_recv)
            pl.when(sends)(copy.wait_send)

    depth = lax.rem(lax.broadcasted_iota(jnp.int32, (own, CHUNK), 1), NZ)
    ups = [jnp.where(depth < NZ - m, coeffs[m], 0.0).astype(F32) for m in range(1, 5)]
    downs = [jnp.where(depth >= m, coeffs[m], 0.0).astype(F32) for m in range(1, 5)]

    def to_right(x):
        return remote(phi.at[x, 0], phi.at[x, 1], ring_send.at[0, x], ring_recv.at[0, x], "band", right)

    def to_left(x):
        return remote(phi.at[x, 0], phi.at[x, 2], ring_send.at[1, x], ring_recv.at[1, x], "band", left)

    def place(i):
        return lax.rem(i + 4, planes)

    def hamiltonian(x, starts):
        for start in starts:
            s = WIDTH + start
            center = grid[x + 4, :, pl.ds(s, CHUNK)]
            total = 3.0 * coeffs[0] * center
            for m in range(1, 5):
                total = total + coeffs[m] * (
                    grid[x + 4 + m, :, pl.ds(s, CHUNK)] + grid[x + 4 - m, :, pl.ds(s, CHUNK)]
                )
            for m in (2, 4):
                total = total + coeffs[m] * (
                    grid[x + 4, :, pl.ds(s + m * NZ, CHUNK)] + grid[x + 4, :, pl.ds(s - m * NZ, CHUNK)]
                )
            odd = None
            for m in (1, 3):
                term = coeffs[m] * (
                    grid[x + 4, :, pl.ds(s + m * NZ - 64, CHUNK + 128)]
                    + grid[x + 4, :, pl.ds(s - m * NZ - 64, CHUNK + 128)]
                )
                odd = term if odd is None else odd + term
            total = total + pltpu.roll(odd, CHUNK + 64, axis=1)[:, :CHUNK]
            for m in range(1, 5):
                total = total + ups[m - 1] * pltpu.roll(center, CHUNK - m, axis=1)
                total = total + downs[m - 1] * pltpu.roll(center, m, axis=1)
            weight = potential[pl.ds(x, 1), pl.ds(start, CHUNK)]
            phi[x, 0, :, pl.ds(start, CHUNK)] = weight * center - 2.0 * total

    def send_part(x, first, size):
        part = pl.ds(first, size)
        for side in range(2):
            remote(
                phi.at[x, 0, :, part], phi.at[x, 1 + side, :, part],
                ring_send.at[side, x], ring_recv.at[side, x], "band", (right, left)[side],
            ).start()

    def inside(i, carry):
        hamiltonian(place(i), range(WIDTH, cells - WIDTH, CHUNK))
        return carry

    def send_inside(i, carry):
        send_part(place(i), WIDTH, cells - 2 * WIDTH)
        return carry

    def edges(i, carry):
        x = place(i)
        for first in (0, cells - WIDTH):
            hamiltonian(x, range(first, first + WIDTH, CHUNK))
        for first in (0, cells - WIDTH):
            send_part(x, first, WIDTH)
        return carry

    def whole(i, carry):
        x = place(i)
        hamiltonian(x, range(0, cells, CHUNK))
        to_right(x).start()
        to_left(x).start()
        return carry

    fill.wait()
    fill_weights.wait()
    lax.fori_loop(0, planes - 8, inside, 0)
    pl.semaphore_wait(barrier, nx + ny + nb - 3)
    depart(halos[:4])
    lax.fori_loop(0, planes - 8, send_inside, 0)
    arrive(halos[:2])
    depart(halos[4:])
    lax.fori_loop(0, planes - 8, edges, 0)
    arrive(halos[2:])
    lax.fori_loop(planes - 8, planes, whole, 0)

    def relay_right(x):
        return remote(phi.at[x, 1], phi.at[x, 3], relay_send.at[x], relay_recv.at[x], "band", right)

    def relay_left(x):
        return remote(phi.at[x, 2], phi.at[x, 3], relay_send.at[x], relay_recv.at[x], "band", left)

    relays = (relay_right, relay_left)
    product[...] = jnp.zeros_like(product)
    pairs = planes // 2
    near = 3 * own
    early_rows, late_rows, gram_rows = pl.ds(0, 2 * near), pl.ds(2 * near, 2 * own), pl.ds(2 * count, 2 * count)

    def gather_near(i, carry):
        x, slot = place(i), lax.rem(i, 2)
        stage(x, slot).wait()
        stacked[x] = halves(staged[slot])

        @pl.when(i < planes - 2)
        def _():
            stage(place(i + 2), slot).start()

        to_right(x).wait_recv()
        to_left(x).wait_recv()
        product[early_rows, :] += dot_nt(stacked_halves(phi[x, 0:3].reshape(near, cells)), stacked[x])
        return carry

    def start_relays(i, carry):
        for k in range(2):
            relays[k](place(2 * i + k)).start()
        return carry

    def gather_far(i, carry):
        for k in range(2):
            x = place(2 * i + k)
            relays[k](x).wait()
            to_right(x).wait_send()
            to_left(x).wait_send()
            product[late_rows, :] += dot_nt(stacked_halves(phi[x, 3]), stacked[x])
        return carry

    def sum_start(at, axis, me, n, value):
        rows = pl.ds(0, value.shape[0])
        slots[at, me, rows] = value
        for k in range(1, n):
            sum_copy(at, axis, me, n, rows, k).start()

    def sum_copy(at, axis, me, n, rows, k):
        return remote(
            slots.at[at, me, rows], slots.at[at, me, rows],
            sum_send.at[at, k - 1], sum_recv.at[at, k - 1], axis, lax.rem(me + k, n),
        )

    def sum_finish(at, axis, me, n, size):
        rows = pl.ds(0, size)
        for k in range(1, n):
            sum_copy(at, axis, me, n, rows, k).wait()
        value = slots[at, 0, rows]
        for k in range(1, n):
            value = value + slots[at, k, rows]
        return value

    lax.fori_loop(0, planes - 2, gather_near, 0)
    lax.fori_loop(0, pairs - 1, start_relays, 0)
    lax.fori_loop(planes - 2, planes, gather_near, 0)
    start_relays(pairs - 1, 0)

    scale = 1.0 / ncells
    lane = lax.broadcasted_iota(jnp.int32, (own, 128), 1)
    folded = product[pl.ds(0, near), :] + product[pl.ds(near, near), :]
    folded = folded + pltpu.roll(folded, 64, axis=1)
    first = jnp.where(lane < 64, folded[:own], folded[own : 2 * own])
    sum_start(0, "gx", gx, nx, jnp.concatenate([first, folded[2 * own :]], axis=0))
    gather_far(0, 0)
    sum_start(1, "gy", gy, ny, sum_finish(0, "gx", gx, nx, 2 * own))
    gather_far(1, 0)
    packed = sum_finish(1, "gy", gy, ny, 2 * own) * scale
    first, third = packed[:own], packed[own:]
    other = pltpu.roll(first, 64, axis=1)
    near_weights = stacked_halves(
        jnp.concatenate([jnp.where(lane < 64, first, other), jnp.where(lane < 64, other, first), third], axis=0)
    )

    def removed_near(x, store):
        for start in range(0, cells, WIDE):
            both = dot(near_weights, stacked[x, :, pl.ds(start, WIDE)])
            store(pl.ds(start, WIDE), (both[:near] + both[near:]).reshape(3, own, WIDE))

    def across_copy(side, p, j):
        return remote(
            opposite.at[p, ((2, 0), (1, 3))[side][j]], opposite_in.at[side, p, j],
            opp_send.at[side, p, j], opp_recv.at[side, p, j], "band", (right, left)[side],
        )

    def side_copy(side, p, r):
        return remote(
            sides.at[side, p, r], sides_in.at[side, p, ((1, 3, 0, 2), (2, 0, 3, 1))[side][r]],
            side_send.at[side, p, r], side_recv.at[side, p, ((1, 3, 0, 2), (2, 0, 3, 1))[side][r]],
            "band", (right, left)[side],
        )

    def send_across(p, carry):
        def store(at, value):
            opposite[p, 0:3, :, at] = value

        removed_near(across * quarter + p, store)
        for side, j in ((0, 0), (0, 1), (1, 0)):
            across_copy(side, p, j).start()
        return carry

    def send_direct(p, carry):
        for side in range(2):

            def store(at, value, side=side):
                sides[side, p, 0:3, :, at] = value

            removed_near((right, left)[side] * quarter + p, store)
            side_copy(side, p, 2).start()
        return carry

    def add_and_send(side, p, j):
        across_copy(side, p, j).wait()
        sides[side, p, j] += opposite_in[side, p, j]
        side_copy(side, p, j).start()

    def relay_sums(p, carry):
        for side, j in ((1, 0), (0, 0), (0, 1)):
            add_and_send(side, p, j)
        return carry

    lax.fori_loop(0, quarter, send_across, 0)
    lax.fori_loop(0, quarter, send_direct, 0)
    lax.fori_loop(2, pairs, gather_far, 0)
    folded = product[pl.ds(2 * near, own), :] + product[pl.ds(2 * near + own, own), :]
    sum_start(5, "gx", gx, nx, folded + pltpu.roll(folded, 64, axis=1))
    lax.fori_loop(0, quarter - 1, relay_sums, 0)
    sum_start(6, "gy", gy, ny, sum_finish(5, "gx", gx, nx, own))
    lax.fori_loop(quarter - 1, quarter, relay_sums, 0)
    far_weights = stacked_halves(sum_finish(6, "gy", gy, ny, own) * scale)

    def removed_far(x, store):
        for start in range(0, cells, WIDE):
            both = dot(far_weights, stacked[x, :, pl.ds(start, WIDE)])
            store(pl.ds(start, WIDE), both[:own] + both[own:])

    def send_across_far(p, carry):
        def store(at, value):
            opposite[p, 3, :, at] = value

        removed_far(across * quarter + p, store)
        across_copy(1, p, 1).start()
        return carry

    def send_direct_far(p, carry):
        for side in range(2):

            def store(at, value, side=side):
                sides[side, p, 3, :, at] = value

            removed_far((right, left)[side] * quarter + p, store)
            side_copy(side, p, 3).start()
        return carry

    def relay_sums_far(p, carry):
        add_and_send(1, p, 1)
        return carry

    def own_part(p, carry):
        x = band * quarter + p

        def store(at, value):
            projected[p, 0:3, :, at] = phi[x, 0:3, :, at] - value

        def store_far(at, value):
            projected[p, 3, :, at] = phi[x, 3, :, at] - value

        removed_near(x, store)
        removed_far(x, store_far)
        return carry

    lax.fori_loop(0, quarter, send_across_far, 0)
    lax.fori_loop(0, quarter, send_direct_far, 0)
    lax.fori_loop(0, quarter, relay_sums_far, 0)
    lax.fori_loop(0, quarter, own_part, 0)
    slabs = (band, left, right, across)

    def inner_products(p, carry):
        for side in range(2):
            for r in range(4):
                side_copy(side, p, r).wait_send()
                side_copy(side, p, r).wait_recv()
        for r in range(4):
            result[p, slabs[r]] = projected[p, r] - (sides_in[0, p, r] + sides_in[1, p, r])
        for start in range(0, cells, WIDE):
            at = pl.ds(start, WIDE)
            pieces[p, :, at] = halves(result[p, :, :, at].reshape(count, WIDE))
        both = pieces[p]
        product[gram_rows, pl.ds(0, 2 * count)] += dot_nt(both, both)
        return carry

    lax.fori_loop(0, quarter, inner_products, 0)

    folded = product[pl.ds(2 * count, count), :] + product[pl.ds(3 * count, count), :]
    folded = folded + pltpu.roll(folded, 128 - count, axis=1)
    folded = jnp.where(lax.broadcasted_iota(jnp.int32, folded.shape, 1) < count, folded, 0.0)
    folded = folded + pltpu.roll(folded, count, axis=1)
    folded = folded + pltpu.roll(folded, 2 * count, axis=1)
    packed = pack(folded, 4)
    for entry in ((2, "gx", gx, nx), (3, "gy", gy, ny), (4, "band", band, nb)):
        sum_start(*entry, packed)
        packed = sum_finish(*entry, own)
    inverse = halves(inverse_factor(unpack(packed, 4) * scale))[:, : 2 * count]

    split = cells // 2

    def back(p, side):
        peer = (right, left)[side]
        return remote(
            result.at[p, peer], out.at[band * quarter + p], back_send.at[side, p], back_recv.at[side, p], "band", peer
        )

    def first_hop(p, side):
        part = pl.ds(side * split, split)
        return remote(
            result.at[p, across, :, part], passing.at[side, p],
            hop_send.at[side, p], hop_recv.at[side, p], "band", (right, left)[side],
        )

    def second_hop(p, side):
        part = pl.ds(side * split, split)
        return remote(
            passing.at[side, p], out.at[(left, right)[side] * quarter + p, :, part],
            last_send.at[side, p], last_recv.at[side, p], "band", (right, left)[side],
        )

    def keep(p):
        return pltpu.make_async_copy(result.at[p, band], out.at[band * quarter + p], local_sem.at[p])

    def finish(p, carry):
        for start in range(0, cells, WIDE):
            at = pl.ds(start, WIDE)
            both = dot(inverse, pieces[p, :, at])
            result[p, :, :, at] = (both[:count] + both[count:]).reshape(nb, own, WIDE)
        for side in range(2):
            first_hop(p, side).start()
        for side in range(2):
            back(p, side).start()
        keep(p).start()
        return carry

    lax.fori_loop(0, quarter, finish, 0)

    def forward(p, carry):
        for side in range(2):
            first_hop(p, side).wait()
            second_hop(p, side).start()
        return carry

    lax.fori_loop(0, quarter, forward, 0)

    def drain(p, carry):
        for side in range(2):
            back(p, side).wait()
            second_hop(p, side).wait()
        keep(p).wait()
        return carry

    lax.fori_loop(0, quarter, drain, 0)


def shards(sizes, block, prior, potential):
    nx, ny, nb = sizes
    block_x, prior_x = block.transpose(1, 0, 2), prior.transpose(1, 0, 2)
    planes, own, cells = block_x.shape
    priors, count, quarter = prior_x.shape[1], own * nb, planes // nb
    ncells = planes * nx * cells * ny
    dma = pltpu.SemaphoreType.DMA
    most = max(sizes)
    out = pl.pallas_call(
        functools.partial(kernel, sizes, ncells),
        out_shape=jax.ShapeDtypeStruct(block_x.shape, F32),
        in_specs=[
            pl.BlockSpec(memory_space=pltpu.HBM),
            pl.BlockSpec(memory_space=pltpu.HBM),
            pl.BlockSpec(memory_space=pltpu.HBM),
        ],
        out_specs=pl.BlockSpec(memory_space=pl.ANY),
        scratch_shapes=[
            pltpu.VMEM((planes, cells), F32),
            pltpu.VMEM((planes + 8, own, cells + 2 * WIDTH), F32),
            pltpu.VMEM((planes, nb, own, cells), F32),
            pltpu.VMEM((2, priors, cells), F32),
            pltpu.VMEM((planes, 2 * priors, cells), BF16),
            pltpu.VMEM((4 * count, 128), F32),
            pltpu.VMEM((quarter, nb, own, cells), F32),
            pltpu.VMEM((2, quarter, nb, own, cells), F32),
            pltpu.VMEM((2, quarter, 2, own, cells), F32),
            pltpu.VMEM((2, quarter, nb, own, cells), F32),
            pltpu.VMEM((quarter, nb, own, cells), F32),
            pltpu.VMEM((quarter, 2 * count, cells), BF16),
            pltpu.VMEM((quarter, nb, own, cells), F32),
            pltpu.VMEM((2, quarter, own, cells // 2), F32),
            pltpu.VMEM((7, most, 2 * own, 128), F32),
            dma((quarter,)),
            dma((2,)),
            dma((8,)),
            dma((8,)),
            dma((2, planes)),
            dma((2, planes)),
            dma((planes,)),
            dma((planes,)),
            dma((2, quarter, 2)),
            dma((2, quarter, 2)),
            dma((2, quarter, nb)),
            dma((2, quarter, nb)),
            dma((7, most)),
            dma((7, most)),
            *[dma((2, quarter))] * 6,
        ],
        compiler_params=pltpu.CompilerParams(
            collective_id=0, has_side_effects=True, vmem_limit_bytes=53000000
        ),
    )(block_x, prior_x, potential)
    return out.transpose(1, 0, 2)


def solution(mesh):
    sizes = tuple(mesh.shape[a] for a in ("gx", "gy", "band"))
    in_specs = (P("band", "gx", "gy"), P("band", "gx", "gy"), P("gx", "gy"))
    out_specs = P("band", "gx", "gy")
    return jax.shard_map(
        functools.partial(shards, sizes), mesh=mesh, in_specs=in_specs, out_specs=out_specs, check_vma=False
    )
```
